256 devices in a mesh: blk: 8 (over z), lat: 4 (over x), depth: 8 (over y, core).
Axes of the slice: x: 4, y: 4, z: 8, core: 2. Of those that a mesh axis runs over, the one named last changes fastest.
Arguments:
- face_len: int32 [8, 4, 8, 6], P('blk', 'lat', 'depth'), may hold values from 0 to 128, as said below
- residual: float32 [8, 4, 8, 768, 512], P('blk', 'lat', 'depth'), as said below
- prev_direction: float32 [8, 4, 8, 768, 512], P('blk', 'lat', 'depth'), as said below
- prev_rho: float32 [512], replicated, may hold values from 0.5 to 4
- schur: float32 [8, 4, 8, 768, 768], P('blk', 'lat', 'depth'), as said below
- neumann: float32 [8, 4, 8, 768, 768], P('blk', 'lat', 'depth'), as said below
- coarse_basis: float32 [8, 4, 8, 768, 256], P('blk', 'lat', 'depth'), may hold values from -0.21875 to 0.21875
- coarse_inverse: float32 [8, 4, 8, 256, 256], P('blk', 'lat', 'depth'), as said below
- prim_owner: int32 [8, 4, 8, 256, 1], P('blk', 'lat', 'depth'), may hold values from 0 to 31; in each aligned block of 256 rows (0 to 255, 256 to 511, ..., all dimensions but the last counted through in order) at most 24 rows name the same one
- coarse_row: int32 [8, 4, 8, 256], P('blk', 'lat', 'depth'), may hold values from 0 to 255
Outputs:
- new_residual: float32 [8, 4, 8, 768, 512], P('blk', 'lat', 'depth')
- direction: float32 [8, 4, 8, 768, 512], P('blk', 'lat', 'depth')
- rho_now: float32 [512], replicated
- step_alpha: float32 [512], replicated
- res_norm: float32 [512], replicated
The draws below stay inside these ranges and needn't reach their ends.
Inputs may be any that keep to these rules, and one draw needn't show every extreme that they name: `face_len`: two subdomains that share a face have equal lengths on it; faces on the outer ends of lat and depth have length 0. `residual`: the two copies of a shared interface row are equal, and rows past a face's length are zero. `prev_direction`: the two copies of a shared interface row are equal, and rows past a face's length are zero. `schur`: each matrix has a positive definite symmetric part. `neumann`: each matrix has a positive definite symmetric part. `coarse_inverse`: each matrix has a positive definite symmetric part. `prim_owner`: at most 24 primal dofs of one subdomain have the same owner.
All inputs are finite; a program needn't handle non-finite values.
Results may differ from the reference program's by a relative error of at most 0.00005.
Values sent between devices are 32-bit elements; how exact they have to be, the bound alone decides.
A program may use at most 64 MiB of HBM per device.

```python
import math
import jax
import jax.numpy as jnp
import numpy as np
from jax import lax

F = 128
NB = 768
NR = 512
NC = 256
CO = 256
CAP = 24
N_BLK = 8
N_LAT = 4
N_DEPTH = 8


def face_lengths(base_key):
    seed_key = jax.random.fold_in(base_key, 7)
    key_list = jax.random.split(seed_key, 3)
    full_shape = (N_BLK, N_LAT, N_DEPTH)
    pair_list = []
    for number in range(3):
        drawn_len = F - jax.random.randint(key_list[number], full_shape, 0, F // 2 + 1)
        pair_list.append(drawn_len.astype(jnp.int32))
    cycle_pairs = pair_list[0].at[0, 0, 0].set(F)
    lateral_pairs = pair_list[1].at[:, N_LAT - 1, :].set(0)
    depth_pairs = pair_list[2].at[:, :, N_DEPTH - 1].set(0)
    face_list = [jnp.roll(cycle_pairs, 1, axis=0), cycle_pairs, jnp.roll(lateral_pairs, 1, axis=1), lateral_pairs, jnp.roll(depth_pairs, 1, axis=2), depth_pairs]
    return jnp.stack(face_list, axis=-1)


def shared_field(base_key, salt):
    lengths = face_lengths(base_key)
    seed_key = jax.random.fold_in(base_key, salt)
    key_list = jax.random.split(seed_key, 4)
    full_shape = (N_BLK, N_LAT, N_DEPTH, F, NR)
    position = (jnp.arange(N_BLK)[:, None, None] * (N_LAT * N_DEPTH) + jnp.arange(N_LAT)[None, :, None] * N_DEPTH + jnp.arange(N_DEPTH)[None, None, :]).astype(jnp.float32)
    ramp_scale = 1.0 + 2.0 * position / (N_BLK * N_LAT * N_DEPTH - 1)
    pair_list = []
    for number in range(3):
        raw_values = jax.random.normal(key_list[number], full_shape, jnp.float32)
        pair_list.append(raw_values * ramp_scale[:, :, :, None, None])
    cycle_pairs, lateral_pairs, depth_pairs = pair_list
    face_list = [jnp.roll(cycle_pairs, 1, axis=0), cycle_pairs, jnp.roll(lateral_pairs, 1, axis=1), lateral_pairs, jnp.roll(depth_pairs, 1, axis=2), depth_pairs]
    stacked = jnp.stack(face_list, axis=3)
    live_mask = (jnp.arange(F)[None, None, None, None, :] < lengths[..., None]).astype(jnp.float32)
    return (stacked * live_mask[..., None]).reshape(N_BLK, N_LAT, N_DEPTH, 6 * F, NR)


def dominant(seed_key, order_n):
    key_list = jax.random.split(seed_key, 3)
    leading = (N_BLK, N_LAT, N_DEPTH)
    row_index = jnp.arange(order_n)[:, None]
    col_index = jnp.arange(order_n)[None, :]
    dense_part = jax.random.uniform(key_list[0], leading + (order_n, order_n), jnp.float32, -1.0, 1.0) * (0.4 / order_n)
    band_part = jax.random.uniform(key_list[1], leading + (order_n, order_n), jnp.float32, -1.0, 1.0) * 0.25
    band_part = jnp.where(jnp.abs(row_index - col_index) == 1, band_part, 0.0)
    off_diag = jnp.where(row_index == col_index, 0.0, dense_part) + band_part
    diagonal_part = 1.0 + 0.5 * jax.random.uniform(key_list[2], leading + (order_n,), jnp.float32)
    matrix = off_diag + jnp.where(row_index == col_index, 1.0, 0.0) * diagonal_part[..., :, None]
    return matrix


def draw_face_len(key, part):
    return face_lengths(key)


def draw_residual(key, part):
    return shared_field(key, 21)


def draw_prev_direction(key, part):
    return shared_field(key, 22)


def draw_schur(key, part):
    return dominant(jax.random.fold_in(key, 31), 6 * F)


def draw_neumann(key, part):
    return dominant(jax.random.fold_in(key, 32), 6 * F)


def draw_coarse_inverse(key, part):
    return dominant(jax.random.fold_in(key, 33), CO)


def set_ends(values, stream_key, least, top_value):
    dims = values.shape
    place = [jax.random.randint(jax.random.fold_in(stream_key, axis), (), 0, dims[axis]) for axis in range(len(dims))]
    values = values.at[tuple(place)].set(least)
    longest = dims.index(max(dims))
    place[longest] = (place[longest] + 1) % dims[longest]
    return values.at[tuple(place)].set(top_value)


def steps_of(own_key, dims, pieces, low, top_value):
    loudness, own = 1.0, jax.random.fold_in(own_key, 6)
    for axis_at, blocks in pieces:
        heights = jnp.exp(jax.random.uniform(jax.random.fold_in(own, axis_at), (blocks,), jnp.float32, low / len(pieces), top_value / len(pieces)))
        loudness = loudness * jnp.repeat(heights, dims[axis_at] // blocks).reshape([-1 if axis == axis_at else 1 for axis in range(len(dims))])
    return loudness


def deal_out(stream_key, own, number, rows, amount, top, bound, slope):
    sequence = jax.random.permutation(stream_key, amount)
    heavy_load, common = load_shares(amount, rows * top, bound, slope, True), load_shares(amount, rows * top, bound, slope, False)
    places = jnp.arange(amount)

    def named(sizes, offset_by):
        used = int((sizes > 0).sum())
        fixed = max(1, used // 4)
        moved = fixed + (places - fixed + offset_by * (used - fixed)) % max(1, amount - fixed)
        return jnp.zeros((amount,), jnp.int32).at[sequence[jnp.where(places < fixed, places, moved)]].set(jnp.asarray(sizes, jnp.int32))

    sizes = jnp.where(number % 4 == 0, named(heavy_load, number // 4), named(common, number - number // 4 - 1))
    mixed = jax.random.permutation(jax.random.fold_in(own, 3), amount)
    source_of, receiver = mixed[0:amount // 2 * 2:2], mixed[1:amount // 2 * 2:2]
    room = jnp.minimum(sizes[source_of] - 1, bound - sizes[receiver]) // 2
    room = jnp.where((source_of == sequence[0]) | (receiver == sequence[0]) | (sizes[receiver] == 0), 0, jnp.maximum(room, 0))
    moved = jax.random.randint(jax.random.fold_in(own, 4), (amount // 2,), 0, 1 << 20) % (room + 1)
    sizes = sizes.at[source_of].add(-moved).at[receiver].add(moved)
    labels = jnp.searchsorted(jnp.cumsum(sizes), jnp.arange(rows * top), side="right").astype(jnp.int32)
    grid = labels.reshape(top, rows).T
    grid = grid[jax.random.permutation(jax.random.fold_in(own, 1), rows)]
    offset_by = jax.random.randint(jax.random.fold_in(own, 2), (rows, 1), 0, top)
    return jnp.take_along_axis(grid, (jnp.arange(top)[None, :] + offset_by) % top, axis=1)


def load_shares(count, total, limit, slope, full):
    portions = [(1 << 20) // math.isqrt(standing ** slope) + 1 for standing in range(1, count + 1)]
    largest = limit if full else min(limit, max(-(-total // count), total * portions[0] // sum(portions)))
    least = 1 if total - largest >= count - 1 else 0
    given, spare = [largest] + [least] * (count - 1), total - largest - least * (count - 1)
    while spare > 0:
        free = [i for i in range(1, count) if given[i] < largest] or [i for i in range(1, count) if given[i] < limit]
        pool, budget = sum([portions[i] for i in free]), spare
        for i in free:
            more = min(limit - given[i], max(1, budget * portions[i] // pool), spare)
            given[i] = given[i] + more
            spare = spare - more
    return np.array(given)


def normal_values(own_key, dims, width, reach, pieces=(), kind=jnp.bfloat16):
    drawn = jax.random.normal(own_key, dims, jnp.float32) * width
    if len(pieces) > 0:
        drawn = steps_of(own_key, dims, pieces, -0.22, 0.18) * drawn
    return jnp.clip(drawn, min=-reach, max=reach).astype(kind)


def setup_inputs(seed: int = 0) -> dict:
    arg_keys = jax.random.split(jax.random.key(seed), 11)
    face_len = draw_face_len(jax.random.fold_in(arg_keys[10], 71), 0)
    residual = draw_residual(jax.random.fold_in(arg_keys[10], 71), 0)
    prev_direction = draw_prev_direction(jax.random.fold_in(arg_keys[10], 71), 0)
    prev_rho = jnp.clip(jnp.exp(jax.random.uniform(arg_keys[3], (NR,), jnp.float32, math.log(0.5), math.log(4.0))), 0.5, 4.0)
    schur = draw_schur(jax.random.fold_in(arg_keys[10], 71), 0)
    neumann = draw_neumann(jax.random.fold_in(arg_keys[10], 71), 0)
    coarse_basis = normal_values(arg_keys[6], (N_BLK, N_LAT, N_DEPTH, NB, NC), NB ** -0.5, 0.21875, ((0, 8), (1, 4), (2, 8)), jnp.float32)
    coarse_inverse = draw_coarse_inverse(jax.random.fold_in(arg_keys[10], 71), 0)
    prim_owner_keys = jax.random.split(jax.random.fold_in(arg_keys[8], 1), N_BLK * N_LAT * N_DEPTH * NC // NC)
    prim_owner_turns = jax.random.permutation(jax.random.fold_in(arg_keys[8], 3), N_BLK * N_LAT * N_DEPTH * NC // NC)
    prim_owner = jax.vmap(lambda own, number: deal_out(jax.random.fold_in(arg_keys[8], 2), own, number, NC, N_BLK * N_LAT, 1, CAP, 1))(prim_owner_keys, prim_owner_turns).reshape((N_BLK, N_LAT, N_DEPTH, NC, 1))
    coarse_row = set_ends(jax.random.randint(arg_keys[9], (N_BLK, N_LAT, N_DEPTH, NC), 0, CO), jax.random.fold_in(arg_keys[9], 1), 0, CO - 1).astype(jnp.int32)
    return dict(face_len=face_len, residual=residual, prev_direction=prev_direction, prev_rho=prev_rho, schur=schur, neumann=neumann, coarse_basis=coarse_basis, coarse_inverse=coarse_inverse, prim_owner=prim_owner, coarse_row=coarse_row)


exact_mode = lax.Precision.HIGHEST


def live_rows(face_len):
    positions = jnp.arange(F, dtype=jnp.int32)
    live_mask = (positions[None, None, None, None, :] < face_len[..., None]).astype(jnp.float32)
    return live_mask.reshape(N_BLK, N_LAT, N_DEPTH, 6 * F, 1)


def across(vector):
    face_list = vector.reshape(N_BLK, N_LAT, N_DEPTH, 6, F, -1)
    empty_lat = jnp.zeros_like(face_list[:, :1, :, 0])
    empty_dep = jnp.zeros_like(face_list[:, :, :1, 0])
    received = [jnp.roll(face_list[:, :, :, 1], 1, axis=0),
                jnp.roll(face_list[:, :, :, 0], -1, axis=0),
                jnp.concatenate([empty_lat, face_list[:, :-1, :, 3]], axis=1),
                jnp.concatenate([face_list[:, 1:, :, 2], empty_lat], axis=1),
                jnp.concatenate([empty_dep, face_list[:, :, :-1, 5]], axis=2),
                jnp.concatenate([face_list[:, :, 1:, 4], empty_dep], axis=2)]
    return jnp.stack(received, axis=3).reshape(vector.shape)


def batched(matrices, vectors):
    return jnp.einsum("abcnm,abcmr->abcnr", matrices, vectors, precision=exact_mode)


def reference(face_len, residual, prev_direction, prev_rho, schur, neumann, coarse_basis, coarse_inverse, prim_owner, coarse_row):
    live_mask = live_rows(face_len)
    residual_live = live_mask * residual
    weighted = 0.5 * residual_live
    local_part = batched(neumann, weighted)
    coarse_terms = jnp.einsum("abcnk,abcnr->abckr", coarse_basis, weighted, precision=exact_mode)
    owners = N_BLK * N_LAT
    depth_of = jnp.broadcast_to(jnp.arange(N_DEPTH, dtype=jnp.int32)[None, None, :, None], (N_BLK, N_LAT, N_DEPTH, NC))
    slot_ids = ((depth_of * owners + prim_owner[..., 0]) * CO + coarse_row).astype(jnp.int32).reshape(-1)
    coarse_sum = jax.ops.segment_sum(coarse_terms.reshape(-1, NR), slot_ids, num_segments=N_DEPTH * owners * CO)
    blocks = coarse_sum.reshape(N_DEPTH, owners, CO, NR)
    inverse = jnp.transpose(coarse_inverse, (2, 0, 1, 3, 4)).reshape(N_DEPTH, owners, CO, CO)
    solved = jnp.einsum("dopq,doqr->dopr", inverse, blocks, precision=exact_mode).reshape(-1, NR)
    correction = jnp.take(solved, slot_ids, axis=0).reshape(N_BLK, N_LAT, N_DEPTH, NC, NR)
    precond_image = local_part + jnp.einsum("abcnk,abckr->abcnr", coarse_basis, correction, precision=exact_mode)
    precond = 0.5 * live_mask * (precond_image + across(precond_image))
    norm_scale = 0.5 / (N_BLK * N_LAT * N_DEPTH * 6 * F)
    rho_now = norm_scale * jnp.sum(residual_live * precond, axis=(0, 1, 2, 3))
    direction = precond + (rho_now / prev_rho) * (live_mask * prev_direction)
    schur_image = batched(schur, direction)
    applied = live_mask * (schur_image + across(schur_image))
    curvature_value = norm_scale * jnp.sum(direction * applied, axis=(0, 1, 2, 3))
    step_alpha = rho_now / curvature_value
    new_residual = residual_live - step_alpha * applied
    res_norm = norm_scale * jnp.sum(new_residual * new_residual, axis=(0, 1, 2, 3))
    return (new_residual, direction, rho_now, step_alpha, res_norm)
```

```python
import functools
import jax
import jax.numpy as jnp
from jax import lax
from jax.experimental import pallas as pl
from jax.experimental.pallas import tpu as pltpu
from jax.sharding import PartitionSpec as P

CAP = 24
STRIDE = 32
F32 = jnp.float32
BF16 = jnp.bfloat16
MESH = pl.DeviceIdType.MESH


def split(x):
    hi = x.astype(BF16)
    return hi, (x - hi.astype(F32)).astype(BF16)


def mm(a, b):
    return lax.dot_general(a, b, (((1,), (0,)), ((), ())), preferred_element_type=F32)


def mm3(a, bh, bl):
    ah, al = split(a)
    return mm(ah, bh) + (mm(ah, bl) + mm(al, bh))


def iota(shape, dim):
    return lax.broadcasted_iota(jnp.int32, shape, dim)


def step_kernel(
    sizes,
    norm_scale,
    fl_ref,
    own_ref,
    crow_ref,
    prho_ref,
    r_hbm,
    pp_hbm,
    s_hbm,
    n_hbm,
    phi_hbm,
    c_hbm,
    nr_hbm,
    dir_hbm,
    rho_ref,
    alpha_ref,
    norm_ref,
    r_v,
    pp_v,
    s_v,
    n_v,
    phi_v,
    c_v,
    wh_v,
    wl_v,
    th_v,
    tl_v,
    slotr_v,
    slotc_v,
    pick_v,
    pickt_v,
    rows_out,
    rows_in,
    out_buf,
    in_buf,
    rel1,
    ans_buf,
    ret_buf,
    rel2,
    gath_v,
    nloc_v,
    img_v,
    rx1,
    p_v,
    simg_v,
    rx2,
    ar_src,
    ar_a,
    ar_b,
    ar_mid,
    ld_sem,
    row_s,
    row_r,
    x_s,
    x_r,
    rel_s,
    rel_r,
    fwd_s,
    ara_s,
    ara_r,
    arb_s,
    arb_r,
    f_s,
    f_r,
    own_sem,
    o_sem,
):
    n_blk, n_lat, n_depth = sizes
    owners = n_blk * n_lat
    b, l, d = lax.axis_index("blk"), lax.axis_index("lat"), lax.axis_index("depth")
    me = b * n_lat + l
    nb, nr = r_v.shape
    face = nb // 6
    nc = phi_v.shape[1]
    co = c_v.shape[0]
    half = n_blk // 2
    quarter = n_blk // 4

    def load(src, dst, k):
        return pltpu.make_async_copy(src, dst, ld_sem.at[k])

    loads = [
        load(r_hbm, r_v, 0),
        load(phi_hbm, phi_v, 1),
        load(n_hbm, n_v, 2),
        load(c_hbm, c_v, 3),
        load(pp_hbm, pp_v, 4),
        load(s_hbm, s_v, 5),
    ]
    for one in loads:
        one.start()

    in_buf[:, CAP:, :] = jnp.zeros((owners, STRIDE - CAP, nr), F32)

    def peer(k):
        db, j = k // n_lat, k % n_lat
        return lax.rem(b + db, n_blk), lax.rem(l + j, n_lat)

    barrier = pltpu.get_barrier_semaphore()

    def greet(k, c):
        pb, plat = peer(k)
        pl.semaphore_signal(barrier, inc=1, device_id=(pb, plat, d), device_id_type=MESH)
        return c

    lax.fori_loop(1, owners, greet, 0)

    def greet_depth(k, c):
        pl.semaphore_signal(
            barrier, inc=1, device_id=(b, l, lax.rem(d + k, n_depth)), device_id_type=MESH
        )
        return c

    lax.fori_loop(1, n_depth, greet_depth, 0)

    own_row = own_ref[...]
    own_b = jnp.broadcast_to(own_row.astype(F32), (nc, nc))
    own_t = jnp.transpose(own_b)
    ii, jj = iota((nc, nc), 0), iota((nc, nc), 1)
    same = own_b == own_t
    rank_row = jnp.sum(jnp.where(same & (ii < jj), 1.0, 0.0), axis=0, keepdims=True)
    rank_col = jnp.sum(jnp.where(same & (jj < ii), 1.0, 0.0), axis=1, keepdims=True)
    slotr_v[...] = own_row * CAP + rank_row.astype(jnp.int32)
    slotc_v[...] = (own_t * CAP + rank_col).astype(jnp.int32)
    left = jnp.where(
        jnp.broadcast_to(own_row, (owners, nc)) == iota((owners, nc), 0),
        jnp.broadcast_to((crow_ref[...] + 1).astype(F32), (owners, nc)),
        0.0,
    ).astype(BF16)
    right = jnp.where(
        rank_col.astype(jnp.int32) + STRIDE * l == iota((nc, 4 * STRIDE), 1), 1.0, 0.0
    ).astype(BF16)
    table = mm(left, right)
    for o in range(owners):
        rows_out[o] = table[o : o + 1, :]

    loads[0].wait()
    for f in range(6):
        rows = pl.ds(f * face, face)
        live = iota((face, nr), 0) < fl_ref[f]
        rl = jnp.where(live, r_v[rows, :], 0.0)
        r_v[rows, :] = rl
        wh, wl = split(0.5 * rl)
        wh_v[rows, :] = wh
        wl_v[rows, :] = wl
    loads[1].wait()
    terms = mm3(jnp.transpose(phi_v[...]), wh_v[...], wl_v[...])
    th, tl = split(terms)
    th_v[...] = th
    tl_v[...] = tl

    pl.semaphore_wait(barrier, owners - 1 + n_depth - 1)

    def rows_copy(k, c):
        pb, plat = peer(k)
        pltpu.make_async_remote_copy(
            src_ref=rows_out.at[pb * n_lat + plat],
            dst_ref=rows_in.at[me],
            send_sem=row_s.at[0],
            recv_sem=row_r.at[0],
            device_id=(pb, plat, d),
            device_id_type=MESH,
        ).start()
        return c

    lax.fori_loop(1, owners, rows_copy, 0)
    pltpu.make_async_copy(rows_out.at[me], rows_in.at[me], row_r.at[0]).start()

    def tile_copy(src, dst, way, dev):
        return pltpu.make_async_remote_copy(
            src_ref=src,
            dst_ref=dst,
            send_sem=x_s.at[way],
            recv_sem=x_r.at[way],
            device_id=dev,
            device_id_type=MESH,
        )

    def tile_sends(src_of, dst_of, rel, way, db):
        tb = lax.rem(b + db, n_blk)
        for j in range(n_lat):
            tl_ = lax.rem(l + j, n_lat)
            src = src_of(tb * n_lat + tl_)
            if db == half:
                via = quarter if j < n_lat // 2 else n_blk - quarter
                pltpu.make_async_remote_copy(
                    src_ref=src,
                    dst_ref=rel.at[j],
                    send_sem=rel_s.at[way],
                    recv_sem=rel_r.at[way],
                    device_id=(lax.rem(b + via, n_blk), l, d),
                    device_id_type=MESH,
                ).start()
            elif db == 0 and j == 0:
                pltpu.make_async_copy(src, dst_of(me), x_r.at[way]).start()
            else:
                tile_copy(src, dst_of(me), way, (tb, tl_, d)).start()

    def tile_forward(dst_of, rel, way):
        pltpu.make_async_copy(rel, rel, rel_r.at[way]).wait()
        for j in range(n_lat):
            go = quarter if j < n_lat // 2 else n_blk - quarter
            origin = lax.rem(b + n_blk - go, n_blk) * n_lat + l
            pltpu.make_async_remote_copy(
                src_ref=rel.at[j],
                dst_ref=dst_of(origin),
                send_sem=fwd_s.at[way],
                recv_sem=x_r.at[way],
                device_id=(lax.rem(b + go, n_blk), lax.rem(l + j, n_lat), d),
                device_id_type=MESH,
            ).start()

    order = [half]
    for step in range(half - 1, 0, -1):
        order += [step, n_blk - step]
    order += [0]

    out_of = lambda o: out_buf.at[o]
    in_of = lambda o: in_buf.at[o, pl.ds(0, CAP)]
    ans_of = lambda o: ans_buf.at[o, pl.ds(0, CAP)]
    ret_of = lambda o: ret_buf.at[o]

    chunk = n_lat * CAP
    for db in order:
        tb = lax.rem(b + db, n_blk)
        pack = jnp.where(
            iota((chunk, nc), 0) + tb * chunk == jnp.broadcast_to(slotr_v[...], (chunk, nc)),
            1.0,
            0.0,
        ).astype(BF16)
        tiles = mm(pack, th_v[...]) + mm(pack, tl_v[...])
        out_buf[pl.ds(tb * n_lat, n_lat)] = tiles.reshape(n_lat, CAP, nr)
        tile_sends(out_of, in_of, rel1, 0, db)

    loads[2].wait()

    def local_block(f, acc):
        rows = pl.ds(pl.multiple_of(f * face, face), face)
        y = mm3(n_v[rows, :], wh_v[...], wl_v[...])
        nloc_v[rows, :] = y
        return acc + jnp.sum(r_v[rows, :] * y, axis=0, keepdims=True)

    rho_local = lax.fori_loop(0, 3, local_block, jnp.zeros((1, nr), F32))
    tile_forward(in_of, rel1, 0)
    rho_local = lax.fori_loop(3, 6, local_block, rho_local)
    ar_src[0] = rho_local

    pltpu.make_async_copy(rows_in, rows_in, row_r.at[0]).wait()
    wide = n_lat * STRIDE
    for g in range(n_blk):
        v = rows_in[g * n_lat]
        for j in range(1, n_lat):
            v = v + rows_in[g * n_lat + j]
        v = v - 1.0
        pick_v[:, pl.ds(g * wide, wide)] = jnp.where(
            jnp.broadcast_to(v, (co, wide)) == iota((co, wide), 0).astype(F32), 1.0, 0.0
        ).astype(BF16)
        vt = jnp.transpose(jnp.broadcast_to(v, (wide, wide)))
        for c in range(co // wide):
            pickt_v[g, :, pl.ds(c * wide, wide)] = jnp.where(
                vt == (iota((wide, wide), 1) + c * wide).astype(F32), 1.0, 0.0
            ).astype(BF16)
    loads[3].wait()

    pltpu.make_async_copy(in_of(slice(None)), in_of(slice(None)), x_r.at[0]).wait()
    per = 2 * n_lat
    for g in range(n_blk // 2):
        xh, xl = split(in_buf[pl.ds(g * per, per)].reshape(per * STRIDE, nr))
        pick = pick_v[:, pl.ds(g * 2 * wide, 2 * wide)]
        part = mm(pick, xh) + mm(pick, xl)
        if g == 0:
            gath_v[...] = part
        else:
            gath_v[...] += part
    gathered = gath_v[...]
    gh, gl = split(gathered)
    solved = mm3(c_v[...], gh, gl)
    ar_src[0] += 2.0 * jnp.sum(gathered * solved, axis=0, keepdims=True)
    sh, sl = split(solved)
    th_v[...] = sh
    tl_v[...] = sl

    def reduce_start(k):
        def send(i, c):
            pb, plat = peer(i)
            pltpu.make_async_remote_copy(
                src_ref=ar_src.at[k],
                dst_ref=ar_a.at[k, me],
                send_sem=ara_s.at[k],
                recv_sem=ara_r.at[k],
                device_id=(pb, plat, d),
                device_id_type=MESH,
            ).start()
            return c

        lax.fori_loop(1, owners, send, 0)
        pltpu.make_async_copy(ar_src.at[k], ar_a.at[k, me], ara_r.at[k]).start()

    def reduce_middle(k):
        pltpu.make_async_copy(ar_a.at[k], ar_a.at[k], ara_r.at[k]).wait()
        ar_mid[k] = jnp.sum(ar_a[k], axis=0)

        def send(i, c):
            pltpu.make_async_remote_copy(
                src_ref=ar_mid.at[k],
                dst_ref=ar_b.at[k, d],
                send_sem=arb_s.at[k],
                recv_sem=arb_r.at[k],
                device_id=(b, l, lax.rem(d + i, n_depth)),
                device_id_type=MESH,
            ).start()
            return c

        lax.fori_loop(1, n_depth, send, 0)
        pltpu.make_async_copy(ar_mid.at[k], ar_b.at[k, d], arb_r.at[k]).start()

    def reduce_end(k):
        pltpu.make_async_copy(ar_b.at[k], ar_b.at[k], arb_r.at[k]).wait()
        return jnp.sum(ar_b[k], axis=0)

    reduce_start(0)
    for db in order:
        tb = lax.rem(b + db, n_blk)
        pick = pickt_v[tb]
        tiles = mm(pick, th_v[...]) + mm(pick, tl_v[...])
        ans_buf[pl.ds(tb * n_lat, n_lat)] = tiles.reshape(n_lat, STRIDE, nr)
        tile_sends(ans_of, ret_of, rel2, 1, db)
    tile_forward(ret_of, rel2, 1)
    reduce_middle(0)
    rho_now = norm_scale * reduce_end(0)
    rho_ref[...] = rho_now
    beta = rho_now / prho_ref[...]
    loads[4].wait()
    loads[5].wait()

    pltpu.make_async_copy(ret_buf, ret_buf, x_r.at[1]).wait()
    lanes = 8 * CAP
    for g in range(owners // 8):
        yh, yl = split(ret_buf[pl.ds(g * 8, 8)].reshape(lanes, nr))
        pack_t = jnp.where(slotc_v[:, :lanes] == iota((nc, lanes), 1) + g * lanes, 1.0, 0.0).astype(BF16)
        part = mm(pack_t, yh) + mm(pack_t, yl)
        if g == 0:
            gath_v[...] = part
        else:
            gath_v[...] += part
    ch, cl = split(gath_v[...])
    th_v[...] = ch
    tl_v[...] = cl

    def face_send(src, rx, turn, f):
        step = 1 if f % 2 == 1 else -1
        axis = f // 2
        dev = [b, l, d]
        n = sizes[axis]
        dev[axis] = lax.rem(dev[axis] + n + step, n)
        return pltpu.make_async_remote_copy(
            src_ref=src.at[pl.ds(f * face, face)],
            dst_ref=rx.at[f ^ 1],
            send_sem=f_s.at[turn, f],
            recv_sem=f_r.at[turn, f ^ 1],
            device_id=tuple(dev),
            device_id_type=MESH,
        )

    for f in range(6):
        rows = pl.ds(f * face, face)
        img_v[rows, :] = nloc_v[rows, :] + mm3(phi_v[rows, :], th_v[...], tl_v[...])
        face_send(img_v, rx1, 0, f).start()

    for f in (4, 5, 2, 3, 0, 1):
        rows = pl.ds(f * face, face)
        face_send(img_v, rx1, 0, f ^ 1).wait_recv()
        live = iota((face, nr), 0) < fl_ref[f]
        p = jnp.where(live, 0.5 * (img_v[rows, :] + rx1[f]) + beta * pp_v[rows, :], 0.0)
        p_v[rows, :] = p
        ph, plo = split(p)
        wh_v[rows, :] = ph
        wl_v[rows, :] = plo
    dir_out = pltpu.make_async_copy(p_v, dir_hbm, o_sem.at[0])
    dir_out.start()

    def schur_block(f, acc):
        rows = pl.ds(pl.multiple_of(f * face, face), face)
        y = mm3(s_v[rows, :], wh_v[...], wl_v[...])
        simg_v[rows, :] = y
        return acc + jnp.sum(p_v[rows, :] * y, axis=0, keepdims=True)

    ar_src[1] = lax.fori_loop(0, 6, schur_block, jnp.zeros((1, nr), F32))
    reduce_start(1)
    for f in range(6):
        face_send(simg_v, rx2, 1, f).start()
    reduce_middle(1)
    alpha = rho_now / (norm_scale * (2.0 * reduce_end(1)))
    alpha_ref[...] = alpha

    total = jnp.zeros((1, nr), F32)
    for f in (4, 5, 2, 3, 0, 1):
        rows = pl.ds(f * face, face)
        face_send(simg_v, rx2, 1, f ^ 1).wait_recv()
        live = iota((face, nr), 0) < fl_ref[f]
        q = r_v[rows, :] - alpha * jnp.where(live, simg_v[rows, :] + rx2[f], 0.0)
        nloc_v[rows, :] = q
        total = total + jnp.sum(q * q, axis=0, keepdims=True)
    ar_src[2] = total
    reduce_start(2)
    nr_out = pltpu.make_async_copy(nloc_v, nr_hbm, o_sem.at[1])
    nr_out.start()
    reduce_middle(2)
    norm_ref[...] = norm_scale * reduce_end(2)

    dir_out.wait()
    nr_out.wait()
    most = pl.ds(0, owners - 1)

    def left(src, sem):
        pltpu.make_async_copy(src, src, sem).wait()

    left(rows_out.at[most], row_s.at[0])
    direct = pl.ds(0, owners - 1 - n_lat)
    left(out_buf.at[direct], x_s.at[0])
    left(out_buf.at[direct], x_s.at[1])
    for way, rel in ((0, rel1), (1, rel2)):
        left(rel, rel_s.at[way])
        left(rel, fwd_s.at[way])
    for k in range(3):
        left(ar_a.at[k, most], ara_s.at[k])
        left(ar_b.at[k, pl.ds(0, n_depth - 1)], arb_s.at[k])
    for turn, src, rx in ((0, img_v, rx1), (1, simg_v, rx2)):
        for f in range(6):
            face_send(src, rx, turn, f).wait_send()


def shards(
    face_len,
    residual,
    prev_direction,
    prev_rho,
    schur,
    neumann,
    coarse_basis,
    coarse_inverse,
    prim_owner,
    coarse_row,
):
    nb, nr = residual.shape[3:]
    face = nb // 6
    nc = coarse_basis.shape[4]
    co = coarse_inverse.shape[3]
    sizes = tuple(lax.axis_size(a) for a in ("blk", "lat", "depth"))
    owners = sizes[0] * sizes[1]
    devices = owners * sizes[2]
    norm_scale = 0.5 / (devices * nb)
    vm, sem = pltpu.VMEM, pltpu.SemaphoreType.DMA
    whole = pl.BlockSpec(memory_space=pltpu.VMEM)
    far = pl.BlockSpec(memory_space=pl.ANY)
    big = jax.ShapeDtypeStruct((nb, nr), F32)
    small = jax.ShapeDtypeStruct((1, nr), F32)
    scratch = [
        vm((nb, nr), F32),
        vm((nb, nr), F32),
        vm((nb, nb), F32),
        vm((nb, nb), F32),
        vm((nb, nc), F32),
        vm((co, co), F32),
        vm((nb, nr), BF16),
        vm((nb, nr), BF16),
        vm((nc, nr), BF16),
        vm((nc, nr), BF16),
        vm((1, nc), jnp.int32),
        vm((nc, nc), jnp.int32),
        vm((co, owners * STRIDE), BF16),
        vm((sizes[0], sizes[1] * STRIDE, co), BF16),
        vm((owners, 1, 4 * STRIDE), F32),
        vm((owners, 1, 4 * STRIDE), F32),
        vm((owners, CAP, nr), F32),
        vm((owners, STRIDE, nr), F32),
        vm((sizes[1], CAP, nr), F32),
        vm((owners, STRIDE, nr), F32),
        vm((owners, CAP, nr), F32),
        vm((sizes[1], CAP, nr), F32),
        vm((nc, nr), F32),
        vm((nb, nr), F32),
        vm((nb, nr), F32),
        vm((6, face, nr), F32),
        vm((nb, nr), F32),
        vm((nb, nr), F32),
        vm((6, face, nr), F32),
        vm((3, 1, nr), F32),
        vm((3, owners, 1, nr), F32),
        vm((3, sizes[2], 1, nr), F32),
        vm((3, 1, nr), F32),
        sem((6,)),
        sem((1,)),
        sem((1,)),
        sem((2,)),
        sem((2,)),
        sem((2,)),
        sem((2,)),
        sem((2,)),
        sem((3,)),
        sem((3,)),
        sem((3,)),
        sem((3,)),
        sem((2, 6)),
        sem((2, 6)),
        sem((1,)),
        sem((2,)),
    ]
    new_residual, direction, rho_now, step_alpha, res_norm = pl.pallas_call(
        functools.partial(step_kernel, sizes, norm_scale),
        out_shape=(big, big, small, small, small),
        in_specs=[pl.BlockSpec(memory_space=pltpu.SMEM), whole, whole, whole] + [far] * 6,
        out_specs=(far, far, whole, whole, whole),
        scratch_shapes=scratch,
        compiler_params=pltpu.CompilerParams(
            collective_id=0, has_side_effects=True, vmem_limit_bytes=60 * 1024 * 1024
        ),
    )(
        face_len.reshape(6),
        prim_owner.reshape(1, nc),
        coarse_row.reshape(1, nc),
        prev_rho.reshape(1, nr),
        residual.reshape(nb, nr),
        prev_direction.reshape(nb, nr),
        schur.reshape(nb, nb),
        neumann.reshape(nb, nb),
        coarse_basis.reshape(nb, nc),
        coarse_inverse.reshape(co, co),
    )
    out_shape = (1, 1, 1, nb, nr)
    return (
        new_residual.reshape(out_shape),
        direction.reshape(out_shape),
        rho_now.reshape(nr),
        step_alpha.reshape(nr),
        res_norm.reshape(nr),
    )


def solution(mesh):
    deep = P("blk", "lat", "depth", None, None)
    in_specs = (
        P("blk", "lat", "depth", None),
        deep,
        deep,
        P(),
        deep,
        deep,
        deep,
        deep,
        deep,
        P("blk", "lat", "depth", None),
    )
    out_specs = (deep, deep, P(), P(), P())
    return jax.shard_map(shards, mesh=mesh, in_specs=in_specs, out_specs=out_specs, check_vma=False)
```

```python
import functools
import jax
import jax.numpy as jnp
from jax import lax
from jax.experimental import pallas as pl
from jax.experimental.pallas import tpu as pltpu
from jax.sharding import PartitionSpec as P

CAP = 24
STRIDE = 32
F32 = jnp.float32
BF16 = jnp.bfloat16
MESH = pl.DeviceIdType.MESH


def split(x):
    hi = x.astype(BF16)
    return hi, (x - hi.astype(F32)).astype(BF16)


def mm(a, b):
    return lax.dot_general(a, b, (((1,), (0,)), ((), ())), preferred_element_type=F32)


def mm3(a, bh, bl):
    ah, al = split(a)
    return mm(ah, bh) + (mm(ah, bl) + mm(al, bh))


def iota(shape, dim):
    return lax.broadcasted_iota(jnp.int32, shape, dim)


def step_kernel(
    sizes,
    norm_scale,
    fl_ref,
    own_ref,
    crow_ref,
    prho_ref,
    r_hbm,
    pp_hbm,
    s_hbm,
    n_hbm,
    phi_hbm,
    c_hbm,
    nr_hbm,
    dir_hbm,
    small_ref,
    r_v,
    pp_v,
    s_v,
    n_v,
    phi_v,
    c_v,
    wh_v,
    wl_v,
    th_v,
    tl_v,
    pth_v,
    ptl_v,
    slotr_v,
    slotc_v,
    pick_v,
    pickt_v,
    rows_out,
    rows_in,
    out_buf,
    in_buf,
    ans_buf,
    ret_buf,
    gath_v,
    nloc_v,
    img_v,
    rx1,
    p_v,
    simg_v,
    rx2,
    ar_src,
    ar_a,
    ar_b,
    ar_mid,
    ld_sem,
    row_s,
    row_r,
    x_s,
    x_r,
    ara_s,
    ara_r,
    arb_s,
    arb_r,
    f_s,
    f_r,
    o_sem,
):
    n_blk, n_lat, n_depth = sizes
    owners = n_blk * n_lat
    b, l, d = lax.axis_index("blk"), lax.axis_index("lat"), lax.axis_index("depth")
    me = b * n_lat + l
    nb, nr = r_v.shape
    face = nb // 6
    nc = phi_v.shape[1]
    co = c_v.shape[0]
    half = n_blk // 2

    def load(src, dst, k):
        return pltpu.make_async_copy(src, dst, ld_sem.at[k])

    loads = [
        load(r_hbm, r_v, 0),
        load(phi_hbm, phi_v, 1),
        load(n_hbm, n_v, 2),
        load(c_hbm, c_v, 3),
        load(pp_hbm, pp_v, 4),
        load(s_hbm, s_v, 5),
    ]
    for one in loads:
        one.start()

    hw = nr // 2
    cols = (pl.ds(0, hw), pl.ds(hw, hw))
    for h in range(2):
        in_buf[h, :, CAP:, :] = jnp.zeros((owners, STRIDE - CAP, hw), F32)

    def peer(k):
        db, j = k // n_lat, k % n_lat
        return lax.rem(b + db, n_blk), lax.rem(l + j, n_lat)

    barrier = pltpu.get_barrier_semaphore()

    def greet(k, c):
        pb, plat = peer(k)
        pl.semaphore_signal(barrier, inc=1, device_id=(pb, plat, d), device_id_type=MESH)
        return c

    lax.fori_loop(1, owners, greet, 0)

    def greet_depth(k, c):
        pl.semaphore_signal(
            barrier, inc=1, device_id=(b, l, lax.rem(d + k, n_depth)), device_id_type=MESH
        )
        return c

    lax.fori_loop(1, n_depth, greet_depth, 0)

    own_row = own_ref[...]
    own_b = jnp.broadcast_to(own_row.astype(F32), (nc, nc))
    own_t = jnp.transpose(own_b)
    ii, jj = iota((nc, nc), 0), iota((nc, nc), 1)
    same = own_b == own_t
    rank_row = jnp.sum(jnp.where(same & (ii < jj), 1.0, 0.0), axis=0, keepdims=True)
    rank_col = jnp.sum(jnp.where(same & (jj < ii), 1.0, 0.0), axis=1, keepdims=True)
    slotr_v[...] = own_row * CAP + rank_row.astype(jnp.int32)
    slotc_v[...] = (own_t * CAP + rank_col).astype(jnp.int32)
    left = jnp.where(
        jnp.broadcast_to(own_row, (owners, nc)) == iota((owners, nc), 0),
        jnp.broadcast_to((crow_ref[...] + 1).astype(F32), (owners, nc)),
        0.0,
    ).astype(BF16)
    right = jnp.where(
        rank_col.astype(jnp.int32) + STRIDE * l == iota((nc, 4 * STRIDE), 1), 1.0, 0.0
    ).astype(BF16)
    table = mm(left, right)
    for o in range(owners):
        rows_out[o] = table[o : o + 1, :]

    loads[0].wait()
    for f in range(6):
        rows = pl.ds(f * face, face)
        live = iota((face, nr), 0) < fl_ref[f]
        rl = jnp.where(live, r_v[rows, :], 0.0)
        r_v[rows, :] = rl
        wh, wl = split(0.5 * rl)
        wh_v[rows, :] = wh
        wl_v[rows, :] = wl
    loads[1].wait()
    ph, plo = split(jnp.transpose(phi_v[...]))
    pth_v[...] = ph
    ptl_v[...] = plo

    def coarse_terms(h):
        c = cols[h]
        wh, wl = wh_v[:, c], wl_v[:, c]
        terms = mm(pth_v[...], wh) + (mm(pth_v[...], wl) + mm(ptl_v[...], wh))
        th, tl = split(terms)
        th_v[:, c] = th
        tl_v[:, c] = tl

    coarse_terms(0)

    pl.semaphore_wait(barrier, owners - 1 + n_depth - 1)

    def rows_copy(k, c):
        pb, plat = peer(k)
        pltpu.make_async_remote_copy(
            src_ref=rows_out.at[pb * n_lat + plat],
            dst_ref=rows_in.at[me],
            send_sem=row_s.at[0],
            recv_sem=row_r.at[0],
            device_id=(pb, plat, d),
            device_id_type=MESH,
        ).start()
        return c

    lax.fori_loop(1, owners, rows_copy, 0)
    pltpu.make_async_copy(rows_out.at[me], rows_in.at[me], row_r.at[0]).start()

    def tile_sends(src_of, dst_of, way, h, db):
        tb = lax.rem(b + db, n_blk)
        for j in range(n_lat):
            tl_ = lax.rem(l + j, n_lat)
            src = src_of(h, tb * n_lat + tl_)
            if db == 0 and j == 0:
                pltpu.make_async_copy(src, dst_of(h, me), x_r.at[way, h]).start()
            else:
                pltpu.make_async_remote_copy(
                    src_ref=src,
                    dst_ref=dst_of(h, me),
                    send_sem=x_s.at[way, h],
                    recv_sem=x_r.at[way, h],
                    device_id=(tb, tl_, d),
                    device_id_type=MESH,
                ).start()

    def tile_wait(dst_of, way, h):
        got = dst_of(h, slice(None))
        pltpu.make_async_copy(got, got, x_r.at[way, h]).wait()

    order = [half]
    for step in range(half - 1, 0, -1):
        order += [step, n_blk - step]
    order += [0]

    out_of = lambda h, o: out_buf.at[h, o]
    in_of = lambda h, o: in_buf.at[h, o, pl.ds(0, CAP)]
    ans_of = lambda h, o: ans_buf.at[h, o, pl.ds(0, CAP)]
    ret_of = lambda h, o: ret_buf.at[h, o]

    chunk = n_lat * CAP
    for h in range(2):
        c = cols[h]
        if h:
            coarse_terms(h)
        for db in order:
            tb = lax.rem(b + db, n_blk)
            pack = jnp.where(
                iota((chunk, nc), 0) + tb * chunk == jnp.broadcast_to(slotr_v[...], (chunk, nc)),
                1.0,
                0.0,
            ).astype(BF16)
            tiles = mm(pack, th_v[:, c]) + mm(pack, tl_v[:, c])
            out_buf[h, pl.ds(tb * n_lat, n_lat)] = tiles.reshape(n_lat, CAP, hw)
            tile_sends(out_of, in_of, 0, h, db)

    loads[2].wait()

    def local_block(f, acc):
        rows = pl.ds(pl.multiple_of(f * face, face), face)
        y = mm3(n_v[rows, :], wh_v[...], wl_v[...])
        nloc_v[rows, :] = y
        return acc + jnp.sum(r_v[rows, :] * y, axis=0, keepdims=True)

    ar_src[0] = lax.fori_loop(0, 6, local_block, jnp.zeros((1, nr), F32))

    pltpu.make_async_copy(rows_in, rows_in, row_r.at[0]).wait()
    wide = n_lat * STRIDE
    for g in range(n_blk):
        v = rows_in[g * n_lat]
        for j in range(1, n_lat):
            v = v + rows_in[g * n_lat + j]
        v = v - 1.0
        pick_v[:, pl.ds(g * wide, wide)] = jnp.where(
            jnp.broadcast_to(v, (co, wide)) == iota((co, wide), 0).astype(F32), 1.0, 0.0
        ).astype(BF16)
        vt = jnp.transpose(jnp.broadcast_to(v, (wide, wide)))
        for c in range(co // wide):
            pickt_v[g, :, pl.ds(c * wide, wide)] = jnp.where(
                vt == (iota((wide, wide), 1) + c * wide).astype(F32), 1.0, 0.0
            ).astype(BF16)
    loads[3].wait()

    def reduce_start(k):
        def send(i, c):
            pb, plat = peer(i)
            pltpu.make_async_remote_copy(
                src_ref=ar_src.at[k],
                dst_ref=ar_a.at[k, me],
                send_sem=ara_s.at[k],
                recv_sem=ara_r.at[k],
                device_id=(pb, plat, d),
                device_id_type=MESH,
            ).start()
            return c

        lax.fori_loop(1, owners, send, 0)
        pltpu.make_async_copy(ar_src.at[k], ar_a.at[k, me], ara_r.at[k]).start()

    def reduce_middle(k):
        pltpu.make_async_copy(ar_a.at[k], ar_a.at[k], ara_r.at[k]).wait()
        ar_mid[k] = jnp.sum(ar_a[k], axis=0)

        def send(i, c):
            pltpu.make_async_remote_copy(
                src_ref=ar_mid.at[k],
                dst_ref=ar_b.at[k, d],
                send_sem=arb_s.at[k],
                recv_sem=arb_r.at[k],
                device_id=(b, l, lax.rem(d + i, n_depth)),
                device_id_type=MESH,
            ).start()
            return c

        lax.fori_loop(1, n_depth, send, 0)
        pltpu.make_async_copy(ar_mid.at[k], ar_b.at[k, d], arb_r.at[k]).start()

    def reduce_end(k):
        pltpu.make_async_copy(ar_b.at[k], ar_b.at[k], arb_r.at[k]).wait()
        return jnp.sum(ar_b[k], axis=0)

    per = 2 * n_lat
    for h in range(2):
        c = cols[h]
        tile_wait(in_of, 0, h)
        for g in range(n_blk // 2):
            xh, xl = split(in_buf[h, pl.ds(g * per, per)].reshape(per * STRIDE, hw))
            pick = pick_v[:, pl.ds(g * 2 * wide, 2 * wide)]
            part = mm(pick, xh) + mm(pick, xl)
            if g == 0:
                gath_v[:, c] = part
            else:
                gath_v[:, c] += part
        gathered = gath_v[:, c]
        gh, gl = split(gathered)
        solved = mm3(c_v[...], gh, gl)
        ar_src[0, :, c] += 2.0 * jnp.sum(gathered * solved, axis=0, keepdims=True)
        sh, sl = split(solved)
        th_v[:, c] = sh
        tl_v[:, c] = sl
        if h:
            reduce_start(0)
        for db in order:
            tb = lax.rem(b + db, n_blk)
            pick = pickt_v[tb]
            tiles = mm(pick, th_v[:, c]) + mm(pick, tl_v[:, c])
            ans_buf[h, pl.ds(tb * n_lat, n_lat)] = tiles.reshape(n_lat, STRIDE, hw)
            tile_sends(ans_of, ret_of, 1, h, db)
    reduce_middle(0)
    rho_now = norm_scale * reduce_end(0)
    small_ref[0] = rho_now
    beta = rho_now / prho_ref[...]
    loads[4].wait()
    loads[5].wait()

    def face_copy(src, rx, f, c, ssem, rsem):
        step = 1 if f % 2 == 1 else -1
        axis = f // 2
        dev = [b, l, d]
        n = sizes[axis]
        dev[axis] = lax.rem(dev[axis] + n + step, n)
        return pltpu.make_async_remote_copy(
            src_ref=src.at[pl.ds(f * face, face), c],
            dst_ref=rx.at[f ^ 1, :, c],
            send_sem=ssem.at[f],
            recv_sem=rsem.at[f ^ 1],
            device_id=tuple(dev),
            device_id_type=MESH,
        )

    def image_face(h, f):
        return face_copy(img_v, rx1, f, cols[h], f_s.at[h], f_r.at[h])

    def schur_face(f):
        return face_copy(simg_v, rx2, f, pl.ds(0, nr), f_s.at[2], f_r.at[2])

    lanes = 8 * CAP
    for h in range(2):
        c = cols[h]
        tile_wait(ret_of, 1, h)
        for g in range(owners // 8):
            yh, yl = split(ret_buf[h, pl.ds(g * 8, 8)].reshape(lanes, hw))
            pack_t = jnp.where(
                slotc_v[:, :lanes] == iota((nc, lanes), 1) + g * lanes, 1.0, 0.0
            ).astype(BF16)
            part = mm(pack_t, yh) + mm(pack_t, yl)
            if g == 0:
                gath_v[:, c] = part
            else:
                gath_v[:, c] += part
        ch, cl = split(gath_v[:, c])
        for f in range(6):
            rows = pl.ds(f * face, face)
            img_v[rows, c] = nloc_v[rows, c] + mm3(phi_v[rows, :], ch, cl)
            image_face(h, f).start()

    for h in range(2):
        c = cols[h]
        for f in (4, 5, 2, 3, 0, 1):
            rows = pl.ds(f * face, face)
            image_face(h, f ^ 1).wait_recv()
            live = iota((face, hw), 0) < fl_ref[f]
            p = jnp.where(
                live, 0.5 * (img_v[rows, c] + rx1[f, :, c]) + beta[:, h * hw : (h + 1) * hw] * pp_v[rows, c], 0.0
            )
            p_v[rows, c] = p
            ph, plo = split(p)
            wh_v[rows, c] = ph
            wl_v[rows, c] = plo

        def schur_block(f, acc):
            rows = pl.ds(pl.multiple_of(f * face, face), face)
            y = mm3(s_v[rows, :], wh_v[:, c], wl_v[:, c])
            simg_v[rows, c] = y
            return acc + jnp.sum(p_v[rows, c] * y, axis=0, keepdims=True)

        ar_src[1, :, c] = lax.fori_loop(0, 6, schur_block, jnp.zeros((1, hw), F32))
    dir_out = pltpu.make_async_copy(p_v, dir_hbm, o_sem.at[0])
    dir_out.start()
    reduce_start(1)
    for f in range(6):
        schur_face(f).start()
    reduce_middle(1)
    alpha = rho_now / (norm_scale * (2.0 * reduce_end(1)))
    small_ref[1] = alpha

    total = jnp.zeros((1, nr), F32)
    for f in (4, 5, 2, 3, 0, 1):
        rows = pl.ds(f * face, face)
        schur_face(f ^ 1).wait_recv()
        live = iota((face, nr), 0) < fl_ref[f]
        q = r_v[rows, :] - alpha * jnp.where(live, simg_v[rows, :] + rx2[f], 0.0)
        nloc_v[rows, :] = q
        total = total + jnp.sum(q * q, axis=0, keepdims=True)
    ar_src[2] = total
    reduce_start(2)
    nr_out = pltpu.make_async_copy(nloc_v, nr_hbm, o_sem.at[1])
    nr_out.start()
    reduce_middle(2)
    small_ref[2] = norm_scale * reduce_end(2)

    dir_out.wait()
    nr_out.wait()
    most = pl.ds(0, owners - 1)

    def left(src, sem):
        pltpu.make_async_copy(src, src, sem).wait()

    left(rows_out.at[most], row_s.at[0])
    for way in range(2):
        for h in range(2):
            left(out_buf.at[h, most], x_s.at[way, h])
    for k in range(3):
        left(ar_a.at[k, most], ara_s.at[k])
        left(ar_b.at[k, pl.ds(0, n_depth - 1)], arb_s.at[k])
    for f in range(6):
        image_face(0, f).wait_send()
        image_face(1, f).wait_send()
        schur_face(f).wait_send()


def pass_kernel(q_hbm, p_hbm, small, nr_hbm, dir_hbm, rho_ref, alpha_ref, norm_ref, q_v, p_v, sems):
    parts = 4
    rows = q_v.shape[0] // parts
    ins, outs = [], []
    for k, (src, mid, dst) in enumerate(((p_hbm, p_v, dir_hbm), (q_hbm, q_v, nr_hbm))):
        for i in range(parts):
            at = pl.ds(i * rows, rows)
            ins.append(pltpu.make_async_copy(src.at[at], mid.at[at], sems.at[0, k, i]))
            outs.append(pltpu.make_async_copy(mid.at[at], dst.at[at], sems.at[1, k, i]))
    for one in ins:
        one.start()
    rho_ref[...] = small[0]
    alpha_ref[...] = small[1]
    norm_ref[...] = small[2]
    for got, out in zip(ins, outs):
        got.wait()
        out.start()
    for out in outs:
        out.wait()


def shards(
    face_len,
    residual,
    prev_direction,
    prev_rho,
    schur,
    neumann,
    coarse_basis,
    coarse_inverse,
    prim_owner,
    coarse_row,
):
    nb, nr = residual.shape[3:]
    face = nb // 6
    nc = coarse_basis.shape[4]
    co = coarse_inverse.shape[3]
    sizes = tuple(lax.axis_size(a) for a in ("blk", "lat", "depth"))
    owners = sizes[0] * sizes[1]
    devices = owners * sizes[2]
    norm_scale = 0.5 / (devices * nb)
    vm, sem = pltpu.VMEM, pltpu.SemaphoreType.DMA
    whole = pl.BlockSpec(memory_space=pltpu.VMEM)
    far = pl.BlockSpec(memory_space=pl.ANY)
    big = jax.ShapeDtypeStruct((nb, nr), F32)
    small = jax.ShapeDtypeStruct((1, nr), F32)
    scratch = [
        vm((nb, nr), F32),
        vm((nb, nr), F32),
        vm((nb, nb), F32),
        vm((nb, nb), F32),
        vm((nb, nc), F32),
        vm((co, co), F32),
        vm((nb, nr), BF16),
        vm((nb, nr), BF16),
        vm((nc, nr), BF16),
        vm((nc, nr), BF16),
        vm((nc, nb), BF16),
        vm((nc, nb), BF16),
        vm((1, nc), jnp.int32),
        vm((nc, nc), jnp.int32),
        vm((co, owners * STRIDE), BF16),
        vm((sizes[0], sizes[1] * STRIDE, co), BF16),
        vm((owners, 1, 4 * STRIDE), F32),
        vm((owners, 1, 4 * STRIDE), F32),
        vm((2, owners, CAP, nr // 2), F32),
        vm((2, owners, STRIDE, nr // 2), F32),
        vm((2, owners, STRIDE, nr // 2), F32),
        vm((2, owners, CAP, nr // 2), F32),
        vm((nc, nr), F32),
        vm((nb, nr), F32),
        vm((nb, nr), F32),
        vm((6, face, nr), F32),
        vm((nb, nr), F32),
        vm((nb, nr), F32),
        vm((6, face, nr), F32),
        vm((3, 1, nr), F32),
        vm((3, owners, 1, nr), F32),
        vm((3, sizes[2], 1, nr), F32),
        vm((3, 1, nr), F32),
        sem((6,)),
        sem((1,)),
        sem((1,)),
        sem((2, 2)),
        sem((2, 2)),
        sem((3,)),
        sem((3,)),
        sem((3,)),
        sem((3,)),
        sem((3, 6)),
        sem((3, 6)),
        sem((2,)),
    ]
    q, p, totals = pl.pallas_call(
        functools.partial(step_kernel, sizes, norm_scale),
        out_shape=(big, big, jax.ShapeDtypeStruct((3, 1, nr), F32)),
        in_specs=[pl.BlockSpec(memory_space=pltpu.SMEM), whole, whole, whole] + [far] * 6,
        out_specs=(far, far, whole),
        scratch_shapes=scratch,
        compiler_params=pltpu.CompilerParams(
            collective_id=0, has_side_effects=True, vmem_limit_bytes=60 * 1024 * 1024
        ),
    )(
        face_len.reshape(6),
        prim_owner.reshape(1, nc),
        coarse_row.reshape(1, nc),
        prev_rho.reshape(1, nr),
        residual.reshape(nb, nr),
        prev_direction.reshape(nb, nr),
        schur.reshape(nb, nb),
        neumann.reshape(nb, nb),
        coarse_basis.reshape(nb, nc),
        coarse_inverse.reshape(co, co),
    )
    new_residual, direction, rho_now, step_alpha, res_norm = pl.pallas_call(
        pass_kernel,
        out_shape=(big, big, small, small, small),
        in_specs=[far, far, whole],
        out_specs=(far, far, whole, whole, whole),
        scratch_shapes=[vm((nb, nr), F32), vm((nb, nr), F32), sem((2, 2, 4))],
    )(q, p, totals)
    out_shape = (1, 1, 1, nb, nr)
    return (
        new_residual.reshape(out_shape),
        direction.reshape(out_shape),
        rho_now.reshape(nr),
        step_alpha.reshape(nr),
        res_norm.reshape(nr),
    )


def solution(mesh):
    deep = P("blk", "lat", "depth", None, None)
    in_specs = (
        P("blk", "lat", "depth", None),
        deep,
        deep,
        P(),
        deep,
        deep,
        deep,
        deep,
        deep,
        P("blk", "lat", "depth", None),
    )
    out_specs = (deep, deep, P(), P(), P())
    return jax.shard_map(shards, mesh=mesh, in_specs=in_specs, out_specs=out_specs, check_vma=False)
```

```python
import functools
import jax
import jax.numpy as jnp
from jax import lax
from jax.experimental import pallas as pl
from jax.experimental.pallas import tpu as pltpu
from jax.sharding import PartitionSpec as P

CAP = 24
STRIDE = 32
PARTS = 4
CUTS = (0, 2, 4)
GROUPS = ((0, 2), (2, 4))
F32 = jnp.float32
BF16 = jnp.bfloat16
MESH = pl.DeviceIdType.MESH


def split(x):
    hi = x.astype(BF16)
    return hi, (x - hi.astype(F32)).astype(BF16)


def mm(a, b):
    return lax.dot_general(a, b, (((1,), (0,)), ((), ())), preferred_element_type=F32)


def mm3(a, bh, bl):
    ah, al = split(a)
    return mm(ah, bh) + (mm(ah, bl) + mm(al, bh))


def iota(shape, dim):
    return lax.broadcasted_iota(jnp.int32, shape, dim)


def step_kernel(
    sizes,
    norm_scale,
    fl_ref,
    own_ref,
    crow_ref,
    prho_ref,
    r_hbm,
    pp_hbm,
    s_hbm,
    n_hbm,
    phi_hbm,
    c_hbm,
    nr_hbm,
    dir_hbm,
    small_ref,
    r_v,
    pp_v,
    s_v,
    n_v,
    phi_v,
    c_v,
    wh_v,
    wl_v,
    th_v,
    tl_v,
    pth_v,
    ptl_v,
    slotr_v,
    slotc_v,
    pick_v,
    pickt_v,
    rows_out,
    rows_in,
    out_buf,
    in_buf,
    ans_buf,
    ret_buf,
    gath_v,
    nloc_v,
    img_v,
    rx1,
    p_v,
    simg_v,
    rx2,
    ar_src,
    ar_a,
    ar_b,
    ar_mid,
    ld_sem,
    row_s,
    row_r,
    x_s,
    x_r,
    ara_s,
    ara_r,
    arb_s,
    arb_r,
    f_s,
    f_r,
    o_sem,
):
    n_blk, n_lat, n_depth = sizes
    owners = n_blk * n_lat
    b, l, d = lax.axis_index("blk"), lax.axis_index("lat"), lax.axis_index("depth")
    me = b * n_lat + l
    nb, nr = r_v.shape
    face = nb // 6
    nc = phi_v.shape[1]
    co = c_v.shape[0]

    def load(src, dst, k):
        return pltpu.make_async_copy(src, dst, ld_sem.at[k])

    loads = [
        load(r_hbm, r_v, 0),
        load(phi_hbm, phi_v, 1),
        load(n_hbm, n_v, 2),
        load(c_hbm, c_v, 3),
        load(pp_hbm, pp_v, 4),
        load(s_hbm, s_v, 5),
    ]
    for one in loads:
        one.start()

    part_w = nr // PARTS
    chunks = len(CUTS) - 1
    widths = [(CUTS[h + 1] - CUTS[h]) * part_w for h in range(chunks)]
    cols = [pl.ds(CUTS[h] * part_w, widths[h]) for h in range(chunks)]
    in_buf[:, CAP:, :] = jnp.zeros((owners, STRIDE - CAP, nr), F32)

    at_blk = [b] + [lax.rem(b + k, n_blk) for k in range(1, n_blk)]
    at_lat = [l] + [lax.rem(l + k, n_lat) for k in range(1, n_lat)]
    at_depth = [d] + [lax.rem(d + k, n_depth) for k in range(1, n_depth)]

    def far_first(n):
        return sorted(range(n), key=lambda k: -min(k, n - k))

    order = far_first(n_blk)
    layer = [
        (at_blk[i], at_lat[j], d) for i in order for j in far_first(n_lat) if i or j
    ]
    column = [(b, l, at_depth[k]) for k in range(1, n_depth)]

    barrier = pltpu.get_barrier_semaphore()
    for dev in layer + column:
        pl.semaphore_signal(barrier, inc=1, device_id=dev, device_id_type=MESH)

    own_row = own_ref[...]
    own_b = jnp.broadcast_to(own_row.astype(F32), (nc, nc))
    own_t = jnp.transpose(own_b)
    ii, jj = iota((nc, nc), 0), iota((nc, nc), 1)
    same = own_b == own_t
    rank_row = jnp.sum(jnp.where(same & (ii < jj), 1.0, 0.0), axis=0, keepdims=True)
    rank_col = jnp.sum(jnp.where(same & (jj < ii), 1.0, 0.0), axis=1, keepdims=True)
    slotr_v[...] = own_row * CAP + rank_row.astype(jnp.int32)
    slotc_v[...] = (own_t * CAP + rank_col).astype(jnp.int32)
    left = jnp.where(
        jnp.broadcast_to(own_row, (owners, nc)) == iota((owners, nc), 0),
        jnp.broadcast_to((crow_ref[...] + 1).astype(F32), (owners, nc)),
        0.0,
    ).astype(BF16)
    right = jnp.where(
        rank_col.astype(jnp.int32) + STRIDE * l == iota((nc, 4 * STRIDE), 1), 1.0, 0.0
    ).astype(BF16)
    table = mm(left, right)
    for o in range(owners):
        rows_out[o] = table[o : o + 1, :]

    loads[0].wait()
    for f in range(6):
        rows = pl.ds(f * face, face)
        live = iota((face, nr), 0) < fl_ref[f]
        rl = jnp.where(live, r_v[rows, :], 0.0)
        r_v[rows, :] = rl
        wh, wl = split(0.5 * rl)
        wh_v[rows, :] = wh
        wl_v[rows, :] = wl
    loads[1].wait()
    ph, plo = split(jnp.transpose(phi_v[...]))
    pth_v[...] = ph
    ptl_v[...] = plo

    def coarse_terms(h):
        c = cols[h]
        wh, wl = wh_v[:, c], wl_v[:, c]
        terms = mm(pth_v[...], wh) + (mm(pth_v[...], wl) + mm(ptl_v[...], wh))
        th, tl = split(terms)
        th_v[:, c] = th
        tl_v[:, c] = tl

    coarse_terms(0)

    pl.semaphore_wait(barrier, owners - 1 + n_depth - 1)

    for dev in layer:
        pltpu.make_async_remote_copy(
            src_ref=rows_out.at[dev[0] * n_lat + dev[1]],
            dst_ref=rows_in.at[me],
            send_sem=row_s.at[0],
            recv_sem=row_r.at[0],
            device_id=dev,
            device_id_type=MESH,
        ).start()
    pltpu.make_async_copy(rows_out.at[me], rows_in.at[me], row_r.at[0]).start()

    def tile_sends(src_of, dst_of, way, h, db):
        tb = at_blk[db]
        for j in range(n_lat):
            tl_ = at_lat[j]
            src = src_of(h, tb * n_lat + tl_)
            if db == 0 and j == 0:
                pltpu.make_async_copy(src, dst_of(h, me), x_r.at[way, h]).start()
            else:
                pltpu.make_async_remote_copy(
                    src_ref=src,
                    dst_ref=dst_of(h, me),
                    send_sem=x_s.at[way, h],
                    recv_sem=x_r.at[way, h],
                    device_id=(tb, tl_, d),
                    device_id_type=MESH,
                ).start()

    def tile_wait(dst_of, way, h):
        got = dst_of(h, slice(None))
        pltpu.make_async_copy(got, got, x_r.at[way, h]).wait()

    out_of = lambda h, o: out_buf.at[o, :, cols[h]]
    in_of = lambda h, o: in_buf.at[o, pl.ds(0, CAP), cols[h]]
    ans_of = lambda h, o: ans_buf.at[o, pl.ds(0, CAP), cols[h]]
    ret_of = lambda h, o: ret_buf.at[o, :, cols[h]]

    chunk = n_lat * CAP
    for h in range(chunks):
        c, hw = cols[h], widths[h]
        if h:
            coarse_terms(h)
        for db in order:
            tb = at_blk[db]
            pack = jnp.where(
                iota((chunk, nc), 0) + tb * chunk == jnp.broadcast_to(slotr_v[...], (chunk, nc)),
                1.0,
                0.0,
            ).astype(BF16)
            tiles = mm(pack, th_v[:, c]) + mm(pack, tl_v[:, c])
            out_buf[pl.ds(tb * n_lat, n_lat), :, c] = tiles.reshape(n_lat, CAP, hw)
            tile_sends(out_of, in_of, 0, h, db)

    loads[2].wait()

    def local_block(f, acc):
        rows = pl.ds(pl.multiple_of(f * face, face), face)
        y = mm3(n_v[rows, :], wh_v[...], wl_v[...])
        nloc_v[rows, :] = y
        return acc + jnp.sum(r_v[rows, :] * y, axis=0, keepdims=True)

    ar_src[0] = lax.fori_loop(0, 6, local_block, jnp.zeros((1, nr), F32))

    pltpu.make_async_copy(rows_in, rows_in, row_r.at[0]).wait()
    wide = n_lat * STRIDE
    for g in range(n_blk):
        v = rows_in[g * n_lat]
        for j in range(1, n_lat):
            v = v + rows_in[g * n_lat + j]
        v = v - 1.0
        pick_v[:, pl.ds(g * wide, wide)] = jnp.where(
            jnp.broadcast_to(v, (co, wide)) == iota((co, wide), 0).astype(F32), 1.0, 0.0
        ).astype(BF16)
        vt = jnp.transpose(jnp.broadcast_to(v, (wide, wide)))
        for c in range(co // wide):
            pickt_v[g, :, pl.ds(c * wide, wide)] = jnp.where(
                vt == (iota((wide, wide), 1) + c * wide).astype(F32), 1.0, 0.0
            ).astype(BF16)
    loads[3].wait()

    def reduce_start(k):
        for dev in layer:
            pltpu.make_async_remote_copy(
                src_ref=ar_src.at[k],
                dst_ref=ar_a.at[k, me],
                send_sem=ara_s.at[k],
                recv_sem=ara_r.at[k],
                device_id=dev,
                device_id_type=MESH,
            ).start()
        pltpu.make_async_copy(ar_src.at[k], ar_a.at[k, me], ara_r.at[k]).start()

    def reduce_middle(k):
        pltpu.make_async_copy(ar_a.at[k], ar_a.at[k], ara_r.at[k]).wait()
        ar_mid[k] = jnp.sum(ar_a[k], axis=0)

        for dev in column:
            pltpu.make_async_remote_copy(
                src_ref=ar_mid.at[k],
                dst_ref=ar_b.at[k, d],
                send_sem=arb_s.at[k],
                recv_sem=arb_r.at[k],
                device_id=dev,
                device_id_type=MESH,
            ).start()
        pltpu.make_async_copy(ar_mid.at[k], ar_b.at[k, d], arb_r.at[k]).start()

    def reduce_end(k):
        pltpu.make_async_copy(ar_b.at[k], ar_b.at[k], arb_r.at[k]).wait()
        return jnp.sum(ar_b[k], axis=0)

    per = 2 * n_lat
    for h in range(chunks):
        c, hw = cols[h], widths[h]
        tile_wait(in_of, 0, h)
        for g in range(n_blk // 2):
            xh, xl = split(in_buf[pl.ds(g * per, per), :, c].reshape(per * STRIDE, hw))
            pick = pick_v[:, pl.ds(g * 2 * wide, 2 * wide)]
            part = mm(pick, xh) + mm(pick, xl)
            if g == 0:
                gath_v[:, c] = part
            else:
                gath_v[:, c] += part
        gathered = gath_v[:, c]
        gh, gl = split(gathered)
        solved = mm3(c_v[...], gh, gl)
        ar_src[0, :, c] += 2.0 * jnp.sum(gathered * solved, axis=0, keepdims=True)
        sh, sl = split(solved)
        th_v[:, c] = sh
        tl_v[:, c] = sl
        if h == chunks - 1:
            reduce_start(0)
        for db in order:
            tb = at_blk[db]
            pick = pickt_v[tb]
            tiles = mm(pick, th_v[:, c]) + mm(pick, tl_v[:, c])
            ans_buf[pl.ds(tb * n_lat, n_lat), :, c] = tiles.reshape(n_lat, STRIDE, hw)
            tile_sends(ans_of, ret_of, 1, h, db)
    reduce_middle(0)
    rho_now = norm_scale * reduce_end(0)
    small_ref[0] = rho_now
    beta = rho_now / prho_ref[...]
    loads[4].wait()
    loads[5].wait()

    def face_copy(src, rx, f, c, ssem, rsem):
        step = 1 if f % 2 == 1 else -1
        axis = f // 2
        dev = [b, l, d]
        n = sizes[axis]
        dev[axis] = lax.rem(dev[axis] + n + step, n)
        return pltpu.make_async_remote_copy(
            src_ref=src.at[pl.ds(f * face, face), c],
            dst_ref=rx.at[f ^ 1, :, c],
            send_sem=ssem.at[f],
            recv_sem=rsem.at[f ^ 1],
            device_id=tuple(dev),
            device_id_type=MESH,
        )

    def image_face(h, f):
        return face_copy(img_v, rx1, f, cols[h], f_s.at[h], f_r.at[h])

    def schur_face(f):
        return face_copy(simg_v, rx2, f, pl.ds(0, nr), f_s.at[chunks], f_r.at[chunks])

    lanes = 8 * CAP
    for h in range(chunks):
        c, hw = cols[h], widths[h]
        tile_wait(ret_of, 1, h)
        for g in range(owners // 8):
            yh, yl = split(ret_buf[pl.ds(g * 8, 8), :, c].reshape(lanes, hw))
            pack_t = jnp.where(
                slotc_v[:, :lanes] == iota((nc, lanes), 1) + g * lanes, 1.0, 0.0
            ).astype(BF16)
            part = mm(pack_t, yh) + mm(pack_t, yl)
            if g == 0:
                gath_v[:, c] = part
            else:
                gath_v[:, c] += part
        ch, cl = split(gath_v[:, c])
        for f in range(6):
            rows = pl.ds(f * face, face)
            img_v[rows, c] = nloc_v[rows, c] + mm3(phi_v[rows, :], ch, cl)
            image_face(h, f).start()

    def direction_part(h):
        c, hw = cols[h], widths[h]
        first = CUTS[h] * part_w
        for f in (4, 5, 2, 3, 0, 1):
            rows = pl.ds(f * face, face)
            image_face(h, f ^ 1).wait_recv()
            live = iota((face, hw), 0) < fl_ref[f]
            p = 0.5 * (img_v[rows, c] + rx1[f, :, c]) + beta[:, first : first + hw] * pp_v[rows, c]
            p = jnp.where(live, p, 0.0)
            p_v[rows, c] = p
            ph, plo = split(p)
            wh_v[rows, c] = ph
            wl_v[rows, c] = plo

    done = 0
    for first, last in GROUPS:
        while done < chunks and CUTS[done + 1] <= last:
            direction_part(done)
            done += 1
        c = pl.ds(first * part_w, (last - first) * part_w)

        def schur_block(f, acc, c=c):
            rows = pl.ds(pl.multiple_of(f * face, face), face)
            y = mm3(s_v[rows, :], wh_v[:, c], wl_v[:, c])
            simg_v[rows, c] = y
            return acc + jnp.sum(p_v[rows, c] * y, axis=0, keepdims=True)

        ar_src[1, :, c] = lax.fori_loop(
            0, 6, schur_block, jnp.zeros((1, (last - first) * part_w), F32)
        )
    dir_out = pltpu.make_async_copy(p_v, dir_hbm, o_sem.at[0])
    dir_out.start()
    reduce_start(1)
    for f in range(6):
        schur_face(f).start()
    reduce_middle(1)
    for f in (4, 5, 2, 3, 0, 1):
        rows = pl.ds(f * face, face)
        schur_face(f ^ 1).wait_recv()
        live = iota((face, nr), 0) < fl_ref[f]
        nloc_v[rows, :] = jnp.where(live, simg_v[rows, :] + rx2[f], 0.0)
    alpha = rho_now / (norm_scale * (2.0 * reduce_end(1)))
    small_ref[1] = alpha

    total = jnp.zeros((1, nr), F32)
    for f in range(6):
        rows = pl.ds(f * face, face)
        q = r_v[rows, :] - alpha * nloc_v[rows, :]
        nloc_v[rows, :] = q
        total = total + jnp.sum(q * q, axis=0, keepdims=True)
    ar_src[2] = total
    reduce_start(2)
    nr_out = pltpu.make_async_copy(nloc_v, nr_hbm, o_sem.at[1])
    nr_out.start()
    reduce_middle(2)
    small_ref[2] = norm_scale * reduce_end(2)

    dir_out.wait()
    nr_out.wait()
    most = pl.ds(0, owners - 1)

    def left(src, sem):
        pltpu.make_async_copy(src, src, sem).wait()

    left(rows_out.at[most], row_s.at[0])
    for way in range(2):
        for h in range(chunks):
            left(out_buf.at[most, :, cols[h]], x_s.at[way, h])
    for k in range(3):
        left(ar_a.at[k, most], ara_s.at[k])
        left(ar_b.at[k, pl.ds(0, n_depth - 1)], arb_s.at[k])
    for f in range(6):
        for h in range(chunks):
            image_face(h, f).wait_send()
        schur_face(f).wait_send()


def pass_kernel(q_hbm, p_hbm, small, nr_hbm, dir_hbm, rho_ref, alpha_ref, norm_ref, q_v, p_v, sems):
    parts = 4
    rows = q_v.shape[0] // parts
    ins, outs = [], []
    for k, (src, mid, dst) in enumerate(((p_hbm, p_v, dir_hbm), (q_hbm, q_v, nr_hbm))):
        for i in range(parts):
            at = pl.ds(i * rows, rows)
            ins.append(pltpu.make_async_copy(src.at[at], mid.at[at], sems.at[0, k, i]))
            outs.append(pltpu.make_async_copy(mid.at[at], dst.at[at], sems.at[1, k, i]))
    for one in ins:
        one.start()
    rho_ref[...] = small[0]
    alpha_ref[...] = small[1]
    norm_ref[...] = small[2]
    for got, out in zip(ins, outs):
        got.wait()
        out.start()
    for out in outs:
        out.wait()


def shards(
    face_len,
    residual,
    prev_direction,
    prev_rho,
    schur,
    neumann,
    coarse_basis,
    coarse_inverse,
    prim_owner,
    coarse_row,
):
    nb, nr = residual.shape[3:]
    face = nb // 6
    nc = coarse_basis.shape[4]
    co = coarse_inverse.shape[3]
    sizes = tuple(lax.axis_size(a) for a in ("blk", "lat", "depth"))
    owners = sizes[0] * sizes[1]
    devices = owners * sizes[2]
    norm_scale = 0.5 / (devices * nb)
    vm, sem = pltpu.VMEM, pltpu.SemaphoreType.DMA
    whole = pl.BlockSpec(memory_space=pltpu.VMEM)
    far = pl.BlockSpec(memory_space=pl.ANY)
    hbm = pl.BlockSpec(memory_space=pltpu.HBM)
    big = jax.ShapeDtypeStruct((nb, nr), F32)
    small = jax.ShapeDtypeStruct((1, nr), F32)
    scratch = [
        vm((nb, nr), F32),
        vm((nb, nr), F32),
        vm((nb, nb), F32),
        vm((nb, nb), F32),
        vm((nb, nc), F32),
        vm((co, co), F32),
        vm((nb, nr), BF16),
        vm((nb, nr), BF16),
        vm((nc, nr), BF16),
        vm((nc, nr), BF16),
        vm((nc, nb), BF16),
        vm((nc, nb), BF16),
        vm((1, nc), jnp.int32),
        vm((nc, nc), jnp.int32),
        vm((co, owners * STRIDE), BF16),
        vm((sizes[0], sizes[1] * STRIDE, co), BF16),
        vm((owners, 1, 4 * STRIDE), F32),
        vm((owners, 1, 4 * STRIDE), F32),
        vm((owners, CAP, nr), F32),
        vm((owners, STRIDE, nr), F32),
        vm((owners, STRIDE, nr), F32),
        vm((owners, CAP, nr), F32),
        vm((nc, nr), F32),
        vm((nb, nr), F32),
        vm((nb, nr), F32),
        vm((6, face, nr), F32),
        vm((nb, nr), F32),
        vm((nb, nr), F32),
        vm((6, face, nr), F32),
        vm((3, 1, nr), F32),
        vm((3, owners, 1, nr), F32),
        vm((3, sizes[2], 1, nr), F32),
        vm((3, 1, nr), F32),
        sem((6,)),
        sem((1,)),
        sem((1,)),
        sem((2, len(CUTS) - 1)),
        sem((2, len(CUTS) - 1)),
        sem((3,)),
        sem((3,)),
        sem((3,)),
        sem((3,)),
        sem((len(CUTS), 6)),
        sem((len(CUTS), 6)),
        sem((2,)),
    ]
    q, p, totals = pl.pallas_call(
        functools.partial(step_kernel, sizes, norm_scale),
        out_shape=(big, big, jax.ShapeDtypeStruct((3, 1, nr), F32)),
        in_specs=[pl.BlockSpec(memory_space=pltpu.SMEM), whole, whole, whole] + [hbm] * 6,
        out_specs=(far, far, whole),
        scratch_shapes=scratch,
        compiler_params=pltpu.CompilerParams(
            collective_id=0, has_side_effects=True, vmem_limit_bytes=60 * 1024 * 1024
        ),
    )(
        face_len.reshape(6),
        prim_owner.reshape(1, nc),
        coarse_row.reshape(1, nc),
        prev_rho.reshape(1, nr),
        residual.reshape(nb, nr),
        prev_direction.reshape(nb, nr),
        schur.reshape(nb, nb),
        neumann.reshape(nb, nb),
        coarse_basis.reshape(nb, nc),
        coarse_inverse.reshape(co, co),
    )
    new_residual, direction, rho_now, step_alpha, res_norm = pl.pallas_call(
        pass_kernel,
        out_shape=(big, big, small, small, small),
        in_specs=[far, far, whole],
        out_specs=(far, far, whole, whole, whole),
        scratch_shapes=[vm((nb, nr), F32), vm((nb, nr), F32), sem((2, 2, 4))],
    )(q, p, totals)
    out_shape = (1, 1, 1, nb, nr)
    return (
        new_residual.reshape(out_shape),
        direction.reshape(out_shape),
        rho_now.reshape(nr),
        step_alpha.reshape(nr),
        res_norm.reshape(nr),
    )


def solution(mesh):
    deep = P("blk", "lat", "depth", None, None)
    in_specs = (
        P("blk", "lat", "depth", None),
        deep,
        deep,
        P(),
        deep,
        deep,
        deep,
        deep,
        deep,
        P("blk", "lat", "depth", None),
    )
    out_specs = (deep, deep, P(), P(), P())
    return jax.shard_map(shards, mesh=mesh, in_specs=in_specs, out_specs=out_specs, check_vma=False)
```

```python
import functools
import jax
import jax.numpy as jnp
from jax import lax
from jax.experimental import pallas as pl
from jax.experimental.pallas import tpu as pltpu
from jax.sharding import PartitionSpec as P

CAP = 24
STRIDE = 32
PARTS = 4
CUTS = (0, 2, 4)
GROUPS = ((0, 2), (2, 4))
F32 = jnp.float32
BF16 = jnp.bfloat16
MESH = pl.DeviceIdType.MESH


def split(x):
    hi = x.astype(BF16)
    return hi, (x - hi.astype(F32)).astype(BF16)


def mm(a, b):
    return lax.dot_general(a, b, (((1,), (0,)), ((), ())), preferred_element_type=F32)


def mm3(a, bh, bl):
    ah, al = split(a)
    return mm(ah, bh) + (mm(ah, bl) + mm(al, bh))


def iota(shape, dim):
    return lax.broadcasted_iota(jnp.int32, shape, dim)


def step_kernel(
    sizes,
    norm_scale,
    fl_ref,
    own_ref,
    crow_ref,
    prho_ref,
    r_hbm,
    pp_hbm,
    s_hbm,
    n_hbm,
    phi_hbm,
    c_hbm,
    nr_hbm,
    dir_hbm,
    small_ref,
    r_v,
    pp_v,
    s_v,
    n_v,
    phi_v,
    c_v,
    wh_v,
    wl_v,
    th_v,
    tl_v,
    pth_v,
    ptl_v,
    slotr_v,
    slotc_v,
    pick_v,
    pickt_v,
    rows_out,
    rows_in,
    out_buf,
    in_buf,
    ans_buf,
    ret_buf,
    gath_v,
    nloc_v,
    img_v,
    rx1,
    p_v,
    simg_v,
    rx2,
    ar_src,
    ar_a,
    ar_b,
    ar_mid,
    ld_sem,
    row_s,
    row_r,
    x_s,
    x_r,
    ara_s,
    ara_r,
    arb_s,
    arb_r,
    f_s,
    f_r,
    o_sem,
):
    n_blk, n_lat, n_depth = sizes
    owners = n_blk * n_lat
    b, l, d = lax.axis_index("blk"), lax.axis_index("lat"), lax.axis_index("depth")
    me = b * n_lat + l
    nb, nr = r_v.shape
    face = nb // 6
    nc = phi_v.shape[1]
    co = c_v.shape[0]

    def load(src, dst, k):
        return pltpu.make_async_copy(src, dst, ld_sem.at[k])

    loads = [
        load(r_hbm, r_v, 0),
        load(phi_hbm, phi_v, 1),
        load(n_hbm, n_v, 2),
        load(c_hbm, c_v, 3),
        load(pp_hbm, pp_v, 4),
        load(s_hbm, s_v, 5),
    ]
    for one in loads:
        one.start()

    part_w = nr // PARTS
    chunks = len(CUTS) - 1
    widths = [(CUTS[h + 1] - CUTS[h]) * part_w for h in range(chunks)]
    cols = [pl.ds(CUTS[h] * part_w, widths[h]) for h in range(chunks)]
    in_buf[:, CAP:, :] = jnp.zeros((owners, STRIDE - CAP, nr), F32)

    at_blk = [b] + [lax.rem(b + k, n_blk) for k in range(1, n_blk)]
    at_lat = [l] + [lax.rem(l + k, n_lat) for k in range(1, n_lat)]
    at_depth = [d] + [lax.rem(d + k, n_depth) for k in range(1, n_depth)]

    def far_first(n):
        return sorted(range(n), key=lambda k: -min(k, n - k))

    order = far_first(n_blk)
    layer = [
        (at_blk[i], at_lat[j], d) for i in order for j in far_first(n_lat) if i or j
    ]
    column = [(b, l, at_depth[k]) for k in range(1, n_depth)]

    barrier = pltpu.get_barrier_semaphore()
    for dev in layer + column:
        pl.semaphore_signal(barrier, inc=1, device_id=dev, device_id_type=MESH)

    own_row = own_ref[...]
    own_b = jnp.broadcast_to(own_row.astype(F32), (nc, nc))
    own_t = jnp.transpose(own_b)
    ii, jj = iota((nc, nc), 0), iota((nc, nc), 1)
    same = own_b == own_t
    rank_row = jnp.sum(jnp.where(same & (ii < jj), 1.0, 0.0), axis=0, keepdims=True)
    rank_col = jnp.sum(jnp.where(same & (jj < ii), 1.0, 0.0), axis=1, keepdims=True)
    slotr_v[...] = own_row * CAP + rank_row.astype(jnp.int32)
    slotc_v[...] = (own_t * CAP + rank_col).astype(jnp.int32)
    left = jnp.where(
        jnp.broadcast_to(own_row, (owners, nc)) == iota((owners, nc), 0),
        jnp.broadcast_to((crow_ref[...] + 1).astype(F32), (owners, nc)),
        0.0,
    ).astype(BF16)
    right = jnp.where(
        rank_col.astype(jnp.int32) + STRIDE * l == iota((nc, 4 * STRIDE), 1), 1.0, 0.0
    ).astype(BF16)
    table = mm(left, right)
    for o in range(owners):
        rows_out[o] = table[o : o + 1, :]

    loads[0].wait()
    for f in range(6):
        rows = pl.ds(f * face, face)
        live = iota((face, nr), 0) < fl_ref[f]
        rl = jnp.where(live, r_v[rows, :], 0.0)
        r_v[rows, :] = rl
        wh, wl = split(0.5 * rl)
        wh_v[rows, :] = wh
        wl_v[rows, :] = wl
    loads[1].wait()
    ph, plo = split(jnp.transpose(phi_v[...]))
    pth_v[...] = ph
    ptl_v[...] = plo

    def coarse_terms(h):
        c = cols[h]
        wh, wl = wh_v[:, c], wl_v[:, c]
        terms = mm(pth_v[...], wh) + (mm(pth_v[...], wl) + mm(ptl_v[...], wh))
        th, tl = split(terms)
        th_v[:, c] = th
        tl_v[:, c] = tl

    coarse_terms(0)

    pl.semaphore_wait(barrier, owners - 1 + n_depth - 1)

    for dev in layer:
        pltpu.make_async_remote_copy(
            src_ref=rows_out.at[dev[0] * n_lat + dev[1]],
            dst_ref=rows_in.at[me],
            send_sem=row_s.at[0],
            recv_sem=row_r.at[0],
            device_id=dev,
            device_id_type=MESH,
        ).start()
    pltpu.make_async_copy(rows_out.at[me], rows_in.at[me], row_r.at[0]).start()

    def tile_sends(src_of, dst_of, way, h, db):
        tb = at_blk[db]
        for j in range(n_lat):
            tl_ = at_lat[j]
            src = src_of(h, tb * n_lat + tl_)
            if db == 0 and j == 0:
                pltpu.make_async_copy(src, dst_of(h, me), x_r.at[way, h]).start()
            else:
                pltpu.make_async_remote_copy(
                    src_ref=src,
                    dst_ref=dst_of(h, me),
                    send_sem=x_s.at[way, h],
                    recv_sem=x_r.at[way, h],
                    device_id=(tb, tl_, d),
                    device_id_type=MESH,
                ).start()

    def tile_wait(dst_of, way, h):
        got = dst_of(h, slice(None))
        pltpu.make_async_copy(got, got, x_r.at[way, h]).wait()

    out_of = lambda h, o: out_buf.at[o, :, cols[h]]
    in_of = lambda h, o: in_buf.at[o, pl.ds(0, CAP), cols[h]]
    ans_of = lambda h, o: ans_buf.at[o, pl.ds(0, CAP), cols[h]]
    ret_of = lambda h, o: ret_buf.at[o, :, cols[h]]

    chunk = n_lat * CAP
    for h in range(chunks):
        c, hw = cols[h], widths[h]
        if h:
            coarse_terms(h)
        for db in order:
            tb = at_blk[db]
            pack = jnp.where(
                iota((chunk, nc), 0) + tb * chunk == jnp.broadcast_to(slotr_v[...], (chunk, nc)),
                1.0,
                0.0,
            ).astype(BF16)
            tiles = mm(pack, th_v[:, c]) + mm(pack, tl_v[:, c])
            out_buf[pl.ds(tb * n_lat, n_lat), :, c] = tiles.reshape(n_lat, CAP, hw)
            tile_sends(out_of, in_of, 0, h, db)

    loads[2].wait()

    def local_block(f, acc):
        rows = pl.ds(pl.multiple_of(f * face, face), face)
        y = mm3(n_v[rows, :], wh_v[...], wl_v[...])
        nloc_v[rows, :] = y
        return acc + jnp.sum(r_v[rows, :] * y, axis=0, keepdims=True)

    ar_src[0] = lax.fori_loop(0, 6, local_block, jnp.zeros((1, nr), F32))

    pltpu.make_async_copy(rows_in, rows_in, row_r.at[0]).wait()
    wide = n_lat * STRIDE
    for g in range(n_blk):
        v = rows_in[g * n_lat]
        for j in range(1, n_lat):
            v = v + rows_in[g * n_lat + j]
        v = v - 1.0
        pick_v[:, pl.ds(g * wide, wide)] = jnp.where(
            jnp.broadcast_to(v, (co, wide)) == iota((co, wide), 0).astype(F32), 1.0, 0.0
        ).astype(BF16)
        vt = jnp.transpose(jnp.broadcast_to(v, (wide, wide)))
        for c in range(co // wide):
            pickt_v[g, :, pl.ds(c * wide, wide)] = jnp.where(
                vt == (iota((wide, wide), 1) + c * wide).astype(F32), 1.0, 0.0
            ).astype(BF16)
    loads[3].wait()

    def reduce_start(k):
        for dev in layer:
            pltpu.make_async_remote_copy(
                src_ref=ar_src.at[k],
                dst_ref=ar_a.at[k, me],
                send_sem=ara_s.at[k],
                recv_sem=ara_r.at[k],
                device_id=dev,
                device_id_type=MESH,
            ).start()
        pltpu.make_async_copy(ar_src.at[k], ar_a.at[k, me], ara_r.at[k]).start()

    def reduce_middle(k):
        pltpu.make_async_copy(ar_a.at[k], ar_a.at[k], ara_r.at[k]).wait()
        ar_mid[k] = jnp.sum(ar_a[k], axis=0)

        for dev in column:
            pltpu.make_async_remote_copy(
                src_ref=ar_mid.at[k],
                dst_ref=ar_b.at[k, d],
                send_sem=arb_s.at[k],
                recv_sem=arb_r.at[k],
                device_id=dev,
                device_id_type=MESH,
            ).start()
        pltpu.make_async_copy(ar_mid.at[k], ar_b.at[k, d], arb_r.at[k]).start()

    def reduce_end(k):
        pltpu.make_async_copy(ar_b.at[k], ar_b.at[k], arb_r.at[k]).wait()
        return jnp.sum(ar_b[k], axis=0)

    per = 2 * n_lat
    for h in range(chunks):
        c, hw = cols[h], widths[h]
        tile_wait(in_of, 0, h)
        for g in range(n_blk // 2):
            xh, xl = split(in_buf[pl.ds(g * per, per), :, c].reshape(per * STRIDE, hw))
            pick = pick_v[:, pl.ds(g * 2 * wide, 2 * wide)]
            part = mm(pick, xh) + mm(pick, xl)
            if g == 0:
                gath_v[:, c] = part
            else:
                gath_v[:, c] += part
        gathered = gath_v[:, c]
        gh, gl = split(gathered)
        solved = mm3(c_v[...], gh, gl)
        ar_src[0, :, c] += 2.0 * jnp.sum(gathered * solved, axis=0, keepdims=True)
        sh, sl = split(solved)
        th_v[:, c] = sh
        tl_v[:, c] = sl
        if h == chunks - 1:
            reduce_start(0)
        for db in order:
            tb = at_blk[db]
            pick = pickt_v[tb]
            tiles = mm(pick, th_v[:, c]) + mm(pick, tl_v[:, c])
            ans_buf[pl.ds(tb * n_lat, n_lat), :, c] = tiles.reshape(n_lat, STRIDE, hw)
            tile_sends(ans_of, ret_of, 1, h, db)
    def face_copy(src, rx, f, c, ssem, rsem):
        step = 1 if f % 2 == 1 else -1
        axis = f // 2
        dev = [b, l, d]
        n = sizes[axis]
        dev[axis] = lax.rem(dev[axis] + n + step, n)
        return pltpu.make_async_remote_copy(
            src_ref=src.at[pl.ds(f * face, face), c],
            dst_ref=rx.at[f ^ 1, :, c],
            send_sem=ssem.at[f],
            recv_sem=rsem.at[f ^ 1],
            device_id=tuple(dev),
            device_id_type=MESH,
        )

    def image_face(h, f):
        return face_copy(img_v, rx1, f, cols[h], f_s.at[h], f_r.at[h])

    def schur_face(f):
        return face_copy(simg_v, rx2, f, pl.ds(0, nr), f_s.at[chunks], f_r.at[chunks])

    lanes = 8 * CAP
    for h in range(chunks):
        c, hw = cols[h], widths[h]
        tile_wait(ret_of, 1, h)
        for g in range(owners // 8):
            yh, yl = split(ret_buf[pl.ds(g * 8, 8), :, c].reshape(lanes, hw))
            pack_t = jnp.where(
                slotc_v[:, :lanes] == iota((nc, lanes), 1) + g * lanes, 1.0, 0.0
            ).astype(BF16)
            part = mm(pack_t, yh) + mm(pack_t, yl)
            if g == 0:
                gath_v[:, c] = part
            else:
                gath_v[:, c] += part
        ch, cl = split(gath_v[:, c])
        for f in range(6):
            rows = pl.ds(f * face, face)
            img_v[rows, c] = nloc_v[rows, c] + mm3(phi_v[rows, :], ch, cl)
            image_face(h, f).start()
        if h == 0:
            reduce_middle(0)

    rho_now = norm_scale * reduce_end(0)
    small_ref[0] = rho_now
    beta = rho_now / prho_ref[...]
    loads[4].wait()
    loads[5].wait()

    def direction_part(h):
        c, hw = cols[h], widths[h]
        first = CUTS[h] * part_w
        for f in (4, 5, 2, 3, 0, 1):
            rows = pl.ds(f * face, face)
            image_face(h, f ^ 1).wait_recv()
            live = iota((face, hw), 0) < fl_ref[f]
            p = 0.5 * (img_v[rows, c] + rx1[f, :, c]) + beta[:, first : first + hw] * pp_v[rows, c]
            p = jnp.where(live, p, 0.0)
            p_v[rows, c] = p
            ph, plo = split(p)
            wh_v[rows, c] = ph
            wl_v[rows, c] = plo

    done = 0
    for first, last in GROUPS:
        while done < chunks and CUTS[done + 1] <= last:
            direction_part(done)
            done += 1
        c = pl.ds(first * part_w, (last - first) * part_w)

        def schur_block(f, acc, c=c):
            rows = pl.ds(pl.multiple_of(f * face, face), face)
            y = mm3(s_v[rows, :], wh_v[:, c], wl_v[:, c])
            simg_v[rows, c] = y
            return acc + jnp.sum(p_v[rows, c] * y, axis=0, keepdims=True)

        ar_src[1, :, c] = lax.fori_loop(
            0, 6, schur_block, jnp.zeros((1, (last - first) * part_w), F32)
        )
    dir_out = pltpu.make_async_copy(p_v, dir_hbm, o_sem.at[0])
    dir_out.start()
    reduce_start(1)
    for f in range(6):
        schur_face(f).start()
    reduce_middle(1)
    for f in (4, 5, 2, 3, 0, 1):
        rows = pl.ds(f * face, face)
        schur_face(f ^ 1).wait_recv()
        live = iota((face, nr), 0) < fl_ref[f]
        nloc_v[rows, :] = jnp.where(live, simg_v[rows, :] + rx2[f], 0.0)
    alpha = rho_now / (norm_scale * (2.0 * reduce_end(1)))
    small_ref[1] = alpha

    total = jnp.zeros((1, nr), F32)
    for f in range(6):
        rows = pl.ds(f * face, face)
        q = r_v[rows, :] - alpha * nloc_v[rows, :]
        nloc_v[rows, :] = q
        total = total + jnp.sum(q * q, axis=0, keepdims=True)
    ar_src[2] = total
    reduce_start(2)
    nr_out = pltpu.make_async_copy(nloc_v, nr_hbm, o_sem.at[1])
    nr_out.start()
    reduce_middle(2)
    small_ref[2] = norm_scale * reduce_end(2)

    dir_out.wait()
    nr_out.wait()
    most = pl.ds(0, owners - 1)

    def left(src, sem):
        pltpu.make_async_copy(src, src, sem).wait()

    left(rows_out.at[most], row_s.at[0])
    for way in range(2):
        for h in range(chunks):
            left(out_buf.at[most, :, cols[h]], x_s.at[way, h])
    for k in range(3):
        left(ar_a.at[k, most], ara_s.at[k])
        left(ar_b.at[k, pl.ds(0, n_depth - 1)], arb_s.at[k])
    for f in range(6):
        for h in range(chunks):
            image_face(h, f).wait_send()
        schur_face(f).wait_send()


def pass_kernel(q_ref, p_ref, small, nr_hbm, dir_hbm, rho_ref, alpha_ref, norm_ref, sems):
    moves = [
        pltpu.make_async_copy(q_ref, nr_hbm, sems.at[0]),
        pltpu.make_async_copy(p_ref, dir_hbm, sems.at[1]),
    ]
    for one in moves:
        one.start()
    rho_ref[...] = small[0]
    alpha_ref[...] = small[1]
    norm_ref[...] = small[2]
    for one in moves:
        one.wait()


def shards(
    face_len,
    residual,
    prev_direction,
    prev_rho,
    schur,
    neumann,
    coarse_basis,
    coarse_inverse,
    prim_owner,
    coarse_row,
):
    nb, nr = residual.shape[3:]
    face = nb // 6
    nc = coarse_basis.shape[4]
    co = coarse_inverse.shape[3]
    sizes = tuple(lax.axis_size(a) for a in ("blk", "lat", "depth"))
    owners = sizes[0] * sizes[1]
    devices = owners * sizes[2]
    norm_scale = 0.5 / (devices * nb)
    vm, sem = pltpu.VMEM, pltpu.SemaphoreType.DMA
    whole = pl.BlockSpec(memory_space=pltpu.VMEM)
    far = pl.BlockSpec(memory_space=pl.ANY)
    hbm = pl.BlockSpec(memory_space=pltpu.HBM)
    big = jax.ShapeDtypeStruct((nb, nr), F32)
    small = jax.ShapeDtypeStruct((1, nr), F32)
    scratch = [
        vm((nb, nr), F32),
        vm((nb, nr), F32),
        vm((nb, nb), F32),
        vm((nb, nb), F32),
        vm((nb, nc), F32),
        vm((co, co), F32),
        vm((nb, nr), BF16),
        vm((nb, nr), BF16),
        vm((nc, nr), BF16),
        vm((nc, nr), BF16),
        vm((nc, nb), BF16),
        vm((nc, nb), BF16),
        vm((1, nc), jnp.int32),
        vm((nc, nc), jnp.int32),
        vm((co, owners * STRIDE), BF16),
        vm((sizes[0], sizes[1] * STRIDE, co), BF16),
        vm((owners, 1, 4 * STRIDE), F32),
        vm((owners, 1, 4 * STRIDE), F32),
        vm((owners, CAP, nr), F32),
        vm((owners, STRIDE, nr), F32),
        vm((owners, STRIDE, nr), F32),
        vm((owners, CAP, nr), F32),
        vm((nc, nr), F32),
        vm((nb, nr), F32),
        vm((nb, nr), F32),
        vm((6, face, nr), F32),
        vm((nb, nr), F32),
        vm((nb, nr), F32),
        vm((6, face, nr), F32),
        vm((3, 1, nr), F32),
        vm((3, owners, 1, nr), F32),
        vm((3, sizes[2], 1, nr), F32),
        vm((3, 1, nr), F32),
        sem((6,)),
        sem((1,)),
        sem((1,)),
        sem((2, len(CUTS) - 1)),
        sem((2, len(CUTS) - 1)),
        sem((3,)),
        sem((3,)),
        sem((3,)),
        sem((3,)),
        sem((len(CUTS), 6)),
        sem((len(CUTS), 6)),
        sem((2,)),
    ]
    q, p, totals = pl.pallas_call(
        functools.partial(step_kernel, sizes, norm_scale),
        out_shape=(big, big, jax.ShapeDtypeStruct((3, 1, nr), F32)),
        in_specs=[pl.BlockSpec(memory_space=pltpu.SMEM), whole, whole, whole] + [hbm] * 6,
        out_specs=(far, far, whole),
        scratch_shapes=scratch,
        compiler_params=pltpu.CompilerParams(
            collective_id=0, has_side_effects=True, vmem_limit_bytes=44 * 1024 * 1024
        ),
    )(
        pltpu.with_memory_space_constraint(face_len.reshape(6), pltpu.HBM),
        pltpu.with_memory_space_constraint(prim_owner.reshape(1, nc), pltpu.HBM),
        pltpu.with_memory_space_constraint(coarse_row.reshape(1, nc), pltpu.HBM),
        pltpu.with_memory_space_constraint(prev_rho.reshape(1, nr), pltpu.HBM),
        pltpu.with_memory_space_constraint(residual.reshape(nb, nr), pltpu.HBM),
        pltpu.with_memory_space_constraint(prev_direction.reshape(nb, nr), pltpu.HBM),
        pltpu.with_memory_space_constraint(schur.reshape(nb, nb), pltpu.HBM),
        pltpu.with_memory_space_constraint(neumann.reshape(nb, nb), pltpu.HBM),
        pltpu.with_memory_space_constraint(coarse_basis.reshape(nb, nc), pltpu.HBM),
        pltpu.with_memory_space_constraint(coarse_inverse.reshape(co, co), pltpu.HBM),
    )
    new_residual, direction, rho_now, step_alpha, res_norm = pl.pallas_call(
        pass_kernel,
        out_shape=(big, big, small, small, small),
        in_specs=[far, far, whole],
        out_specs=(hbm, hbm, whole, whole, whole),
        scratch_shapes=[sem((2,))],
        compiler_params=pltpu.CompilerParams(vmem_limit_bytes=4 * 1024 * 1024),
    )(q, p, totals)
    out_shape = (1, 1, 1, nb, nr)
    return (
        new_residual.reshape(out_shape),
        direction.reshape(out_shape),
        rho_now.reshape(nr),
        step_alpha.reshape(nr),
        res_norm.reshape(nr),
    )


def solution(mesh):
    deep = P("blk", "lat", "depth", None, None)
    in_specs = (
        P("blk", "lat", "depth", None),
        deep,
        deep,
        P(),
        deep,
        deep,
        deep,
        deep,
        deep,
        P("blk", "lat", "depth", None),
    )
    out_specs = (deep, deep, P(), P(), P())
    return jax.shard_map(shards, mesh=mesh, in_specs=in_specs, out_specs=out_specs, check_vma=False)
```
